32 devices in a mesh: grp: 2 (over x), gx: 4 (over z), gy: 4 (over y, core).
Axes of the slice: x: 2, y: 2, z: 4, core: 2. Of those that a mesh axis runs over, the one named last changes fastest.
Arguments:
- theta_anomaly: float32 [192, 64, 128], P(('grp', 'gx'), 'gy'), may hold values from -4 to 4
- humidity_ratio: float32 [192, 64, 128], P(('grp', 'gx'), 'gy'), may hold values from 0.6 to 1.4
- zonal_velocity: float32 [192, 64, 128], P(('grp', 'gx'), 'gy'), may hold values from -1.8 to 1.8
- meridional_velocity: float32 [192, 64, 128], P(('grp', 'gx'), 'gy'), may hold values from -1.8 to 1.8
- vertical_velocity: float32 [192, 64, 128], P(('grp', 'gx'), 'gy'), may hold values from -1.8 to 1.8
- patch_processor_map: int32 [8, 4, 8], P(('grp', 'gx'), 'gy'), may hold values from 0 to 3, as said below
- particle_bucket_population: int32 [8, 4, 8], P(('grp', 'gx'), 'gy'), may hold values from 0 to 1024, as said below
- particle_size_quadratic: float32 [8, 4, 8, 1024], P(('grp', 'gx'), 'gy'), may hold values from 0.25 to 4
- represented_number: float32 [8, 4, 8, 1024], P(('grp', 'gx'), 'gy'), may hold values from 0.5 to 2
- particle_location_number: int32 [8, 4, 8, 1024], P(('grp', 'gx'), 'gy'), may hold values from 48 to 6095, as said below
Outputs:
- final_temperature: float32 [192, 64, 128], P(('grp', 'gx'), 'gy')
- final_vapour: float32 [192, 64, 128], P(('grp', 'gx'), 'gy')
- final_east: float32 [192, 64, 128], P(('grp', 'gx'), 'gy')
- final_north: float32 [192, 64, 128], P(('grp', 'gx'), 'gy')
- final_vertical: float32 [192, 64, 128], P(('grp', 'gx'), 'gy')
- final_size_quadratic: float32 [8, 4, 8, 1024], P(('grp', 'gx'), 'gy')
The draws below stay inside these ranges and needn't reach their ends.
Inputs may be any that keep to these rules, and one draw needn't show every extreme that they name: `patch_processor_map`: entry [a, y, b] is the index along gx of the device in the same row (same grp half, same gy) that holds the droplets of column block b of device (a, y). Different blocks of one device go to different owners, so one device sends at most 2 blocks to one owner; in every row some owner holds 2 blocks from every device of the row. `particle_bucket_population`: entry [a, y, r] counts the live droplets of slot r = s x 2 + t of the owner (a, y); they are the first ones of the slot. A slot that receives no block has none; every slot of an owner that holds 2 blocks from every device is full. `particle_location_number`: the cell within the slot's block, column 128 + level, with levels from 48 to 79. Within a slot the live droplets are sorted by column, and so are the others.
All inputs are finite; a program needn't handle non-finite values.
Results may differ from the reference program's by a relative error of at most 0.0003.
Values sent between devices are 32-bit elements; how exact they have to be, the bound alone decides.
A program may use at most 64 MiB of HBM per device.

```python
import math
import jax
import jax.numpy as jnp

CX = 24
VERTICAL_LAYERS = 128
NBD = 8
KLO = 48
KHI = 80
DPB = 1024
NSUB = 4
ITERS = 4
NSTEP = 1
XPEERS = 4
XTILES = 8
YTILES = 4
SPAN_COUNT_EAST = 192
SPAN_COUNT_NORTH = 64
BY = 2
BCOL = 48
SLOTS = 2
ROWSLOTS = 8


def wind_draw(key, salt):
    normals = jnp.clip(jax.random.normal(jax.random.fold_in(key, salt), (SPAN_COUNT_EAST, SPAN_COUNT_NORTH, VERTICAL_LAYERS), jnp.float32), -4.0, 4.0)
    x_place = jnp.arange(SPAN_COUNT_EAST, dtype=jnp.float32)
    y_place = jnp.arange(SPAN_COUNT_NORTH, dtype=jnp.float32)
    x_frac = x_place / max(SPAN_COUNT_EAST - 1, 1)
    y_frac = y_place / max(SPAN_COUNT_NORTH - 1, 1)
    amplitude = 0.05 * jnp.exp(jnp.log(3.0) * (x_frac[:, None] + y_frac[None, :]))
    return amplitude[..., None] * normals


def draw_zonal_velocity(key, part):
    return wind_draw(key, 21)


def draw_meridional_velocity(key, part):
    return wind_draw(key, 22)


def draw_vertical_velocity(key, part):
    return wind_draw(key, 23)


def plan_owners(key):
    groups = XTILES // XPEERS
    busiest = jax.random.randint(jax.random.fold_in(key, 11), (groups, 1, YTILES, 1), 0, XPEERS)
    spread = (NBD + SLOTS - 1) // SLOTS
    offsets = jax.random.randint(jax.random.fold_in(key, 12), (groups, XPEERS, YTILES, 1), 0, spread)
    blocks = jnp.arange(NBD, dtype=jnp.int32)
    owners = (busiest - offsets + blocks // SLOTS) % XPEERS
    return (owners, busiest)


def plan_counts(key):
    owners, busiest = plan_owners(key)
    target = jnp.arange(XPEERS, dtype=jnp.int32)
    slot_index = jnp.arange(SLOTS, dtype=jnp.int32)
    blocks = jnp.arange(NBD, dtype=jnp.int32)
    owner_rows = owners.transpose(0, 2, 1, 3)
    matches = (owner_rows[:, None, :, :, :, None] == target[None, :, None, None, None, None]) & ((blocks % SLOTS)[None, None, None, None, :, None] == slot_index[None, None, None, None, None, :])
    assigned = jnp.any(matches, axis=4)
    drawn_count = jax.random.randint(jax.random.fold_in(key, 13), assigned.shape, DPB // 4, DPB + 1)
    busy_owner = target[None, :, None, None, None] == busiest[..., None]
    counts = jnp.where(assigned, jnp.where(busy_owner, DPB, drawn_count), 0)
    return counts.reshape(XTILES, YTILES, ROWSLOTS)


def draw_patch_processor_map(key, part):
    owners, busiest = plan_owners(key)
    return owners.reshape(XTILES, YTILES, NBD).astype(jnp.int32)


def draw_particle_bucket_population(key, part):
    return plan_counts(key).astype(jnp.int32)


def draw_particle_location_number(key, part):
    counts = plan_counts(key)
    extent = (XTILES, YTILES, ROWSLOTS, DPB)
    column = jax.random.randint(jax.random.fold_in(key, 14), extent, 0, BCOL)
    alive_mask = jnp.arange(DPB, dtype=jnp.int32) < counts[..., None]
    ordered = jnp.sort(jnp.where(alive_mask, column, column + BCOL), axis=-1)
    column = jnp.where(ordered >= BCOL, ordered - BCOL, ordered)
    height = jax.random.randint(jax.random.fold_in(key, 15), extent, KLO, KHI)
    return (column * VERTICAL_LAYERS + height).astype(jnp.int32)


def level_of(key, shape, cuts, smallest, top_value):
    loudness = 1.0
    for dim, parts in cuts:
        draws = jax.random.uniform(jax.random.fold_in(jax.random.fold_in(key, 6), dim), (parts,), jnp.float32, smallest / len(cuts), top_value / len(cuts))
        loudness = loudness * jnp.repeat(jnp.exp(draws), shape[dim] // parts).reshape((-1,) + (1,) * (len(shape) - 1 - dim))
    return loudness


def gaussian(own_key, shape, scale, bound, split=(), kind=jnp.bfloat16):
    values = scale * jax.random.normal(own_key, shape, jnp.float32)
    if split:
        values = values * level_of(own_key, shape, split, -0.22, 0.18)
    return jnp.clip(values, -bound, bound).astype(kind)


def setup_inputs(seed: int = 0) -> dict:
    key_list = jax.random.split(jax.random.key(seed), 11)
    return {
        "theta_anomaly": gaussian(key_list[0], (SPAN_COUNT_EAST, SPAN_COUNT_NORTH, VERTICAL_LAYERS), 1.0, 4.0, ((0, 8), (1, 4)), jnp.float32),
        "humidity_ratio": jnp.clip(0.6 + 0.79999995 * jax.random.uniform(key_list[1], (SPAN_COUNT_EAST, SPAN_COUNT_NORTH, VERTICAL_LAYERS), jnp.float32) ** level_of(key_list[1], (SPAN_COUNT_EAST, SPAN_COUNT_NORTH, VERTICAL_LAYERS), ((0, 8), (1, 4)), -0.2, 0.2), 0.6, 1.4),
        "zonal_velocity": draw_zonal_velocity(jax.random.fold_in(key_list[10], 71), 0),
        "meridional_velocity": draw_meridional_velocity(jax.random.fold_in(key_list[10], 71), 0),
        "vertical_velocity": draw_vertical_velocity(jax.random.fold_in(key_list[10], 71), 0),
        "patch_processor_map": draw_patch_processor_map(jax.random.fold_in(key_list[10], 71), 0),
        "particle_bucket_population": draw_particle_bucket_population(jax.random.fold_in(key_list[10], 71), 0),
        "particle_size_quadratic": jnp.clip(jnp.exp(math.log(4.0) - 2.7725887 * jax.random.uniform(key_list[7], (XTILES, YTILES, ROWSLOTS, DPB), jnp.float32) ** level_of(key_list[7], (XTILES, YTILES, ROWSLOTS, DPB), ((0, 8), (1, 4)), -0.2, 0.2)), 0.25, 4.0),
        "represented_number": jnp.clip(jnp.exp(math.log(2.0) - 1.3862944 * jax.random.uniform(key_list[8], (XTILES, YTILES, ROWSLOTS, DPB), jnp.float32) ** level_of(key_list[8], (XTILES, YTILES, ROWSLOTS, DPB), ((0, 8), (1, 4)), -0.2, 0.2)), 0.5, 2.0),
        "particle_location_number": draw_particle_location_number(jax.random.fold_in(key_list[10], 71), 0),
    }


TIME_INCREMENT = 0.15
THERMAL_LIFT = 0.5
HUMID_LIFT = 0.3
HELMHOLTZ = 0.001
CLAUSIUS_FACTOR = 0.2
GROWTH = 0.5
GROWTH_SLOPE = 0.1
SUB_STEP = 0.25
CURVATURE = 0.05
FLOOR_SQUARE = 0.04
CONDENSE = 0.2
PHASE_WARMING = 2.5

def profiles():
    heights = jnp.arange(VERTICAL_LAYERS, dtype=jnp.float32)
    midpoint_mass_per_volume = jnp.exp(-(heights + 0.5) / VERTICAL_LAYERS)
    interface_mass_per_volume = jnp.where(heights < VERTICAL_LAYERS - 1, jnp.exp(-(heights + 1.0) / VERTICAL_LAYERS), 0.0)
    return (midpoint_mass_per_volume, interface_mass_per_volume)

def level_above(values):
    return jnp.concatenate([values[..., 1:], jnp.zeros_like(values[..., :1])], axis=-1)

def level_below(values):
    return jnp.concatenate([jnp.zeros_like(values[..., :1]), values[..., :-1]], axis=-1)

def beside_all(values):
    return (jnp.roll(values, -1, 0), jnp.roll(values, 1, 0), jnp.roll(values, -1, 1), jnp.roll(values, 1, 1))

def operate(values, midpoint_mass_per_volume, interface_mass_per_volume):
    east_side, west_side, north_side, south_side = beside_all(values)
    return midpoint_mass_per_volume * ((4.0 + HELMHOLTZ) * values - east_side - west_side - north_side - south_side) + interface_mass_per_volume * (values - level_above(values)) + level_below(interface_mass_per_volume) * (values - level_below(values))

def solve_pressure(right_side, midpoint_mass_per_volume, interface_mass_per_volume):
    potential = jnp.zeros_like(right_side)
    residual = right_side
    direction = right_side
    norm_now = jnp.sum(residual * residual)
    for iteration in range(ITERS):
        applied = operate(direction, midpoint_mass_per_volume, interface_mass_per_volume)
        step_length = norm_now / jnp.sum(direction * applied)
        potential = potential + step_length * direction
        residual = residual - step_length * applied
        norm_next = jnp.sum(residual * residual)
        direction = residual + norm_next / norm_now * direction
        norm_now = norm_next
    return potential

def advect_scalars(values, zonal_velocity, meridional_velocity, vertical_velocity):
    east_side, west_side, north_side, south_side = beside_all(values)
    lower_level = jnp.concatenate([values[..., :1], values[..., :-1]], axis=-1)
    upper_level = jnp.concatenate([values[..., 1:], values[..., -1:]], axis=-1)
    tendency = jnp.maximum(zonal_velocity, 0.0) * (values - west_side) + jnp.minimum(zonal_velocity, 0.0) * (east_side - values) + jnp.maximum(meridional_velocity, 0.0) * (values - south_side) + jnp.minimum(meridional_velocity, 0.0) * (north_side - values) + jnp.maximum(vertical_velocity, 0.0) * (values - lower_level) + jnp.minimum(vertical_velocity, 0.0) * (upper_level - values)
    return values - TIME_INCREMENT * tendency

def grow_droplets(supersat_ratio, warmth, particle_size_quadratic, represented_number, alive_mask):
    growth_rate = GROWTH * jnp.exp(GROWTH_SLOPE * warmth)
    square_now = particle_size_quadratic
    for substep in range(NSUB):
        square_now = jnp.maximum(square_now + 2.0 * SUB_STEP * growth_rate * (supersat_ratio - CURVATURE / jnp.sqrt(square_now)), FLOOR_SQUARE)
    grown_square = jnp.where(alive_mask, square_now, particle_size_quadratic)
    mass_change = jnp.where(alive_mask, represented_number * (grown_square * jnp.sqrt(grown_square) - particle_size_quadratic * jnp.sqrt(particle_size_quadratic)), 0.0)
    return (grown_square, mass_change)

def into_patches(values):
    shaped = values.reshape(XTILES, CX, YTILES, NBD, BY, VERTICAL_LAYERS)
    return shaped.transpose(0, 2, 3, 1, 4, 5).reshape(XTILES, YTILES, NBD, BCOL * VERTICAL_LAYERS)

def from_blocks(blocks):
    shaped = blocks.reshape(XTILES, YTILES, NBD, CX, BY, VERTICAL_LAYERS)
    return shaped.transpose(0, 3, 1, 2, 4, 5).reshape(SPAN_COUNT_EAST, SPAN_COUNT_NORTH, VERTICAL_LAYERS)

def reference(theta_anomaly, humidity_ratio, zonal_velocity, meridional_velocity, vertical_velocity, patch_processor_map, particle_bucket_population, particle_size_quadratic, represented_number, particle_location_number):
    midpoint_mass_per_volume, interface_mass_per_volume = profiles()
    tile_x = jnp.arange(XTILES, dtype=jnp.int32)[:, None, None]
    tile_y = jnp.arange(YTILES, dtype=jnp.int32)[None, :, None]
    block_index = jnp.arange(NBD, dtype=jnp.int32)[None, None, :]
    owner_row = (tile_x // XPEERS * XPEERS + patch_processor_map).astype(jnp.int32)
    slot_index = (tile_x % XPEERS * SLOTS + block_index % SLOTS).astype(jnp.int32)
    row_y = jnp.broadcast_to(tile_y, patch_processor_map.shape).astype(jnp.int32)
    block_count = particle_bucket_population[owner_row, row_y, slot_index]
    patch_location = particle_location_number[owner_row, row_y, slot_index]
    block_mult = represented_number[owner_row, row_y, slot_index]
    block_radius = particle_size_quadratic[owner_row, row_y, slot_index]
    alive_mask = jnp.arange(DPB, dtype=jnp.int32) < block_count[..., None]
    offsets = (jnp.arange(XTILES * YTILES * NBD, dtype=jnp.int32) * (BCOL * VERTICAL_LAYERS)).reshape(XTILES, YTILES, NBD, 1)
    flat_cell = (patch_location + offsets).reshape(-1)
    for stepping in range(NSTEP):
        raised_airmass = vertical_velocity + TIME_INCREMENT * (THERMAL_LIFT * theta_anomaly + HUMID_LIFT * humidity_ratio)
        divergence = midpoint_mass_per_volume * ((jnp.roll(zonal_velocity, -1, 0) - jnp.roll(zonal_velocity, 1, 0)) * 0.5 + (jnp.roll(meridional_velocity, -1, 1) - jnp.roll(meridional_velocity, 1, 1)) * 0.5) + 0.5 * (level_above(midpoint_mass_per_volume * raised_airmass) - level_below(midpoint_mass_per_volume * raised_airmass))
        potential = solve_pressure(-divergence / TIME_INCREMENT, midpoint_mass_per_volume, interface_mass_per_volume)
        zonal_velocity = zonal_velocity - TIME_INCREMENT * 0.5 * (jnp.roll(potential, -1, 0) - jnp.roll(potential, 1, 0))
        meridional_velocity = meridional_velocity - TIME_INCREMENT * 0.5 * (jnp.roll(potential, -1, 1) - jnp.roll(potential, 1, 1))
        vertical_velocity = raised_airmass - TIME_INCREMENT * 0.5 * (level_above(potential) - level_below(potential))
        advected_theta = advect_scalars(theta_anomaly, zonal_velocity, meridional_velocity, vertical_velocity)
        advected_humidity = advect_scalars(humidity_ratio, zonal_velocity, meridional_velocity, vertical_velocity)
        supersat_ratio = advected_humidity * jnp.exp(-CLAUSIUS_FACTOR * advected_theta) - 1.0
        sat_drops = jnp.take_along_axis(into_patches(supersat_ratio), patch_location, axis=3)
        grow_particles = jnp.take_along_axis(into_patches(advected_theta), patch_location, axis=3)
        block_radius, mass_change = grow_droplets(sat_drops, grow_particles, block_radius, block_mult, alive_mask)
        liquid_content = CONDENSE * jax.ops.segment_sum(mass_change.reshape(-1), flat_cell, num_segments=XTILES * YTILES * NBD * BCOL * VERTICAL_LAYERS)
        liquid_content = from_blocks(liquid_content.reshape(XTILES, YTILES, NBD, BCOL * VERTICAL_LAYERS))
        theta_anomaly = advected_theta + PHASE_WARMING * liquid_content
        humidity_ratio = advected_humidity - liquid_content
    final_size_quadratic = particle_size_quadratic.at[owner_row, row_y, slot_index].set(block_radius)
    return (theta_anomaly, humidity_ratio, zonal_velocity, meridional_velocity, vertical_velocity, final_size_quadratic)
```

```python
import functools

import jax
import jax.numpy as jnp
from jax import lax
from jax.experimental import pallas as pl
from jax.experimental.pallas import tpu as pltpu
from jax.sharding import PartitionSpec as P

NBD = 8
NSUB = 4
ITERS = 4
KLO = 48
KHI = 80

DT = 0.15
THERMAL_LIFT = 0.5
HUMID_LIFT = 0.3
HELMHOLTZ = 0.001
CLAUSIUS_FACTOR = 0.2
GROWTH = 0.5
GROWTH_SLOPE = 0.1
SUB_STEP = 0.25
CURVATURE = 0.05
FLOOR_SQUARE = 0.04
CONDENSE = 0.2
PHASE_WARMING = 2.5

H = 4
MESH = pl.DeviceIdType.MESH
def sweep(lo, hi, body, k=8):
    turns = (hi - lo) // k

    def turn(i, c):
        for j in range(k):
            body(lo + i * k + j)
        return c

    lax.fori_loop(0, turns, turn, 0)
    for x in range(lo + turns * k, hi):
        body(x)


def cg_coefficients(m):
    def inner(a, b):
        total = None
        for i, ai in enumerate(a):
            part = None
            for j, bj in enumerate(b):
                term = bj * (0.5 * (m[i + j] + m[abs(i - j)]))
                part = term if part is None else part + term
            part = ai * part
            total = part if total is None else total + part
        return total

    one = jnp.ones_like(m[0])
    zero = jnp.zeros_like(m[0])

    def apply(d):
        out = [zero] * (len(d) + 1)
        for i, di in enumerate(d):
            out[i] = out[i] + 6.0 * di
            if i == 0:
                out[1] = out[1] + 6.0 * di
            else:
                out[i + 1] = out[i + 1] + 3.0 * di
                out[i - 1] = out[i - 1] + 3.0 * di
        return out

    res, d, pot, rr = [one], [one], [], m[0]
    for it in range(ITERS):
        img = apply(d)
        alpha = rr / inner(d, img)
        pot = [
            alpha * d[i] + (pot[i] if i < len(pot) else 0.0) for i in range(len(d))
        ]
        if it + 1 == ITERS:
            break
        res = [(res[i] if i < len(res) else zero) - alpha * img[i] for i in range(len(img))]
        new = inner(res, res)
        beta = new / rr
        d = [res[i] + (beta * d[i] if i < len(d) else 0.0) for i in range(len(res))]
        rr = new
    return pot


def kernel(
    ngrp, ngx, ngy, slots,
    t_hbm, q_hbm, u_hbm, v_hbm, w_hbm, map_hbm, cnt_hbm, size_hbm, mult_hbm, cell_hbm,
    to_ref, qo_ref, uo_ref, vo_ref, wo_ref, so_ref,
    us, vs, ws, te, qe, le, p0, p1, p2, p3, phi_s, size_v, mult_v, cell_v, map_s, cnt_s,
    xs, xr, ys, yr, cs, cr, ds, dr, part, got_x,
    blk, packed, pos_s, col_s, size_d, mult_d, sat_s, tmp_s, hot_s, xb, rb, out2, grid_c,
    load_sem, send_sem, recv_sem, sum_send, sum_recv,
):
    cx, cy, nz = t_hbm.shape
    rows = cy + 8
    nt = cy // 8
    grp, gx, gy = lax.axis_index("grp"), lax.axis_index("gx"), lax.axis_index("gy")
    nx = ngrp * ngx
    xt = grp * ngx + gx
    everyone = nx * ngy

    def dev(dx, dy):
        other = lax.rem(xt + dx + nx, nx)
        return (lax.div(other, ngx), lax.rem(other, ngx), lax.rem(gy + dy + ngy, ngy))

    def other(o):
        return dev(lax.div(o, ngy), lax.rem(o, ngy))

    loads = []

    def fetch(src, dst):
        copy = pltpu.make_async_copy(src, dst, load_sem.at[len(loads)])
        copy.start()
        loads.append(copy)

    inside = (pl.ds(1, cx), pl.ds(0, cy))
    fetch(u_hbm, us.at[pl.ds(2, cx)])
    fetch(v_hbm, vs)
    fetch(w_hbm, ws)
    fetch(t_hbm, te.at[inside])
    fetch(q_hbm, qe.at[inside])

    barrier = pltpu.get_barrier_semaphore()

    def greet(o, c):
        pl.semaphore_signal(barrier, inc=1, device_id=other(o), device_id_type=MESH)
        return c

    lax.fori_loop(1, everyone, greet, 0)
    fetch(cell_hbm, cell_v)
    fetch(size_hbm, size_v)
    fetch(mult_hbm, mult_v)
    fetch(cnt_hbm, cnt_s)
    fetch(map_hbm, map_s)

    lane = lax.broadcasted_iota(jnp.int32, (1, nz), 1)
    height = lane.astype(jnp.float32)
    rho = jnp.exp(-(height + 0.5) / nz)
    face = jnp.where(lane < nz - 1, jnp.exp(-(height + 1.0) / nz), 0.0)
    face_dn = jnp.where(lane > 0, jnp.exp(-height / nz), 0.0)
    not_top = jnp.where(lane < nz - 1, 1.0, 0.0)
    not_bot = jnp.where(lane > 0, 1.0, 0.0)
    rho_up = jnp.where(lane < nz - 1, jnp.exp(-(height + 1.5) / nz), 0.0)
    rho_dn = jnp.where(lane > 0, jnp.exp(-(height - 0.5) / nz), 0.0)
    half_r = -0.5 / DT
    rho_h, up_h, down_h = rho * half_r, rho_up * half_r, rho_dn * half_r
    sub = lax.broadcasted_iota(jnp.int32, (8, nz), 0)
    zero8 = jnp.zeros((8, nz), jnp.float32)

    def up(f):
        return pltpu.roll(f, nz - 1, 1)

    def down(f):
        return pltpu.roll(f, 1, 1)

    def north(f):
        return pltpu.roll(f, rows - 1, 0)

    def south(f):
        return pltpu.roll(f, 1, 0)

    def turn(f, s):
        return pltpu.roll(f, s, 0)

    def keep(mask, f):
        return jnp.where(mask, f, 0.0)

    def ends(f):
        return keep((sub == 0) | (sub == 7), f)

    for i in (0, 1, cx + 2, cx + 3):
        us[i] = jnp.zeros((cy, nz), jnp.float32)
    for copy in loads[:5]:
        copy.wait()

    def begin(x):
        tt, qq, vv = te[x + 1, 0:cy, :], qe[x + 1, 0:cy, :], vs[x]
        lift = ws[x] + DT * (THERMAL_LIFT * tt + HUMID_LIFT * qq)
        le[x] = lift
        tall = jnp.concatenate([vv, zero8], axis=0)
        c = rho_h * (north(tall) - south(tall))
        own = c[:cy] + (rho_h * (us[x + 3] - us[x + 1]) + (up_h * up(lift) - down_h * down(lift)))
        c0, c1, c2 = own[:8], own[cy - 8 :], c[cy:]
        p0[x + H, 0:cy, :] = own
        p0[x + H, cy:rows, :] = c2
        t0, t1, q0, q1 = tt[:8], tt[cy - 8 :], qq[:8], qq[cy - 8 :]
        ys[0, x + 1] = jnp.where(
            sub >= 4, c1, jnp.where(sub == 1, turn(t1, 2), jnp.where(sub == 2, turn(q1, 3), c2))
        )
        ys[1, x + 1] = jnp.where(
            sub < 4, c0, jnp.where(sub == 5, turn(t0, 5), jnp.where(sub == 6, turn(q0, 6), c2))
        )

    def rim(x):
        c = rho_h * (us[x + 3] - us[x + 1])
        p0[x + H, 0:cy, :] = c
        ys[0, x + 1] = keep(sub >= 4, c[cy - 8 :])
        ys[1, x + 1] = keep(sub < 4, c[:8])

    rim(-1)
    rim(cx)
    sweep(0, cx, begin)

    for d, first, cols in ((0, cx - 4, (cx - 1, cx - 2, cx - 3)), (1, -1, (0, 1, 2))):
        for k in range(5):
            for i in range(nt):
                xs[d, k * nt + i] = p0[first + k + H, 8 * i : 8 * i + 8, :]
        a, b, c = (p0[x + H, cy:rows, :] for x in cols)
        xs[d, 5 * nt] = jnp.where(
            (sub == 0) | (sub == 7),
            a,
            jnp.where(
                (sub == 1) | (sub == 2), turn(b, 2), keep((sub == 3) | (sub == 4), turn(c, 4))
            ),
        )
    for d, side in ((0, 0), (1, 0), (2, 1), (3, 1)):
        y = [ys[side, cx - 3 + j if d in (0, 2) else 4 - j] for j in range(5)]
        if side == 0:
            cs[d, 0] = jnp.where(sub >= 4, y[4], turn(y[3], 3))
            cs[d, 1] = jnp.where(
                (sub == 0) | (sub >= 6),
                y[2],
                jnp.where(sub == 3, turn(y[0], 3), keep((sub == 1) | (sub == 2), turn(y[1], 2))),
            )
        else:
            cs[d, 0] = jnp.where(sub < 4, y[4], turn(y[3], 5))
            cs[d, 1] = jnp.where(
                (sub == 7) | (sub < 2),
                y[2],
                jnp.where(sub == 4, turn(y[0], 5), keep((sub == 2) | (sub == 3), turn(y[1], 3))),
            )

    pl.semaphore_wait(barrier, everyone - 1)

    started = []

    def send(src, dst, target):
        i = len(started)
        copy = pltpu.make_async_remote_copy(
            src_ref=src, dst_ref=dst, send_sem=send_sem.at[i], recv_sem=recv_sem.at[i],
            device_id=target, device_id_type=MESH,
        )
        copy.start()
        started.append(copy)
        return copy

    def drain():
        for copy in started:
            copy.wait_send()

    halo = [
        send(xs.at[0], xr.at[0], dev(1, 0)),
        send(xs.at[1], xr.at[1], dev(-1, 0)),
        send(cs.at[0], cr.at[0], dev(1, 1)),
        send(cs.at[1], cr.at[1], dev(-1, 1)),
        send(cs.at[2], cr.at[2], dev(1, -1)),
        send(cs.at[3], cr.at[3], dev(-1, -1)),
        send(ys.at[0], yr.at[0], dev(0, 1)),
        send(ys.at[1], yr.at[1], dev(0, -1)),
    ]
    sides = []
    for f in (te, qe):
        for edge, place, dx in ((cx, 0, 1), (1, cx + 1, -1)):
            sides.append(
                send(
                    f.at[pl.ds(edge, 1), pl.ds(0, cy)],
                    f.at[pl.ds(place, 1), pl.ds(0, cy)],
                    dev(dx, 0),
                )
            )

    for copy in loads[5:]:
        copy.wait()
    dpb = size_v.shape[1]
    nrow = ngx * slots
    place_of = lax.broadcasted_iota(jnp.int32, (slots, dpb), 1)
    slot_of = lax.broadcasted_iota(jnp.int32, (slots, dpb), 0)

    def living(o):
        limit = jnp.zeros((slots, dpb), jnp.int32)
        for t in range(slots):
            limit = jnp.where(slot_of == t, cnt_s[0, o * slots + t], limit)
        return place_of < limit

    for o in range(ngx):
        r = slice(o * slots, (o + 1) * slots)
        ds[o, 0] = size_v[r, :]
        ds[o, 1] = jnp.where(living(o), mult_v[r, :], 0.0)
        ds[o, 2] = cell_v[r, :].astype(jnp.float32)
    moves = []
    for o in range(1, ngx):
        peer = lax.rem(gx + o, ngx)
        moves.append(send(ds.at[peer], dr.at[gx], (grp, peer, gy)))
    dr[gx] = ds[gx]

    for copy in halo:
        copy.wait_recv()

    def merge(x):
        a, b = yr[0, x + 1], yr[1, x + 1]
        p0[x + H, 0:8, :] += keep(sub == 0, a)
        p0[x + H, cy - 8 : cy, :] += keep(sub == 7, b)
        p0[x + H, cy:rows, :] += jnp.where(sub < 4, b, a)
        te[x + 1, cy:rows, :] = jnp.where(sub == 7, turn(a, 6), turn(b, 3))
        qe[x + 1, cy:rows, :] = jnp.where(sub == 7, turn(a, 5), turn(b, 2))

    sweep(0, cx, merge)

    for d, ring in ((0, 0), (1, cx + 1)):
        a, b = cr[d, 0], cr[d, 1]
        low = [
            turn(b, 5),
            turn(b, 6),
            b,
            turn(a, 5),
            a,
        ]
        a, b = cr[2 + d, 0], cr[2 + d, 1]
        high = [
            turn(b, 3),
            turn(b, 5),
            b,
            turn(a, 3),
            a,
        ]
        misc = xr[d, 5 * nt]
        for j in range(5):
            x = j - 4 if d == 0 else cx + 3 - j
            k = j if d == 0 else 4 - j
            third = keep((sub >= 8 - j) & (sub >= 4), low[j]) + keep((sub < j) & (sub < 4), high[j])
            tiles = [xr[d, k * nt + i] for i in range(nt)]
            if j < 4:
                tiles[0] = tiles[0] + keep(sub == 0, low[j])
                tiles[nt - 1] = tiles[nt - 1] + keep(sub == 7, high[j])
            if j == 3:
                third = third + ends(misc) + jnp.where(sub < 4, yr[1, ring], yr[0, ring])
            elif j == 2:
                third = third + ends(turn(misc, 6))
            elif j == 1:
                third = third + ends(turn(misc, 4))
            for i in range(nt):
                s = slice(8 * i, 8 * i + 8)
                p0[x + H, s, :] = tiles[i] + p0[x + H, s, :] if j >= 3 else tiles[i]
            s = slice(cy, rows)
            p0[x + H, s, :] = third + p0[x + H, s, :] if j == 4 else third

    diag = ((4.0 + HELMHOLTZ) * rho + face + face_dn) / 6.0 - 1.0
    rho6, face6, face_dn6 = rho / 6.0, face / 6.0, face_dn / 6.0

    def scaled(f, x):
        c = f[x]
        side = f[x + 1] + f[x - 1] + north(c) + south(c)
        return diag * c - rho6 * side - face6 * up(c) - face_dn6 * down(c)

    def step1(x):
        p1[x] = scaled(p0, x)

    def step2(x):
        p2[x] = 2.0 * scaled(p1, x) - p0[x]

    def step3(x):
        p3[x] = 2.0 * scaled(p2, x) - p1[x]

    full = cx + 2 * H
    sweep(1, full - 1, step1)
    sweep(2, full - 2, step2)
    sweep(3, full - 3, step3)

    def dots(x, acc):
        a0, a1, a2, a3 = p0[x, 0:cy, :], p1[x, 0:cy, :], p2[x, 0:cy, :], p3[x]
        a4 = 2.0 * scaled(p3, x)[:cy] - a2
        a3 = a3[:cy]
        pairs = ((a0, a0), (a0, a1), (a1, a1), (a1, a2), (a2, a2), (a2, a3), (a3, a3), (a3, a4))
        return tuple(s + f * g for s, (f, g) in zip(acc, pairs))

    def dots_two(i, acc):
        return dots(H + 2 * i + 1, dots(H + 2 * i, acc))

    acc = lax.fori_loop(0, cx // 2, dots_two, (jnp.zeros((cy, nz), jnp.float32),) * 8)
    if cx % 2:
        acc = dots(H + cx - 1, acc)
    corner = lax.broadcasted_iota(jnp.int32, (8, nz), 0) == lax.broadcasted_iota(
        jnp.int32, (8, nz), 1
    )
    sums = jnp.concatenate([jnp.sum(a, axis=0, keepdims=True) for a in acc], axis=0)
    sums = jnp.sum(sums, axis=1, keepdims=True)
    part[...] = jnp.sum(jnp.where(corner, sums, 0.0), axis=0, keepdims=True)

    def share_start(o, c):
        pltpu.make_async_remote_copy(
            src_ref=part, dst_ref=got_x.at[o - 1], send_sem=sum_send, recv_sem=sum_recv,
            device_id=other(o), device_id_type=MESH,
        ).start()
        return c

    lax.fori_loop(1, everyone, share_start, 0)

    for copy in sides + moves:
        copy.wait_recv()
    half = nz // 2
    nlev = KHI - KLO
    for o in range(ngx):
        r = slice(o * slots, (o + 1) * slots)
        size_d[r, :] = dr[o, 0]
        mult_d[r, :] = dr[o, 1]
        cell = dr[o, 2].astype(jnp.int32)
        col_s[r, :] = cell // (2 * nz)
        pos_s[r, :] = (cell // nz) % 2 * nlev + cell % nz - KLO
    wide = lax.broadcasted_iota(jnp.int32, (half, dpb), 0)
    narrow = lax.broadcasted_iota(jnp.int32, (cx, dpb), 0)
    for r in range(nrow):
        one = jnp.where(wide == pos_s[r : r + 1, :], 1.0, 0.0).astype(jnp.bfloat16)
        hot_s[r, 0:half, :] = one
        hot_s[r, half:nz, :] = one

    pltpu.make_async_copy(got_x, got_x, sum_recv).wait()
    total = part[...]
    for o in range(everyone - 1):
        total = total + got_x[o]
    total = jnp.where(corner, total, 0.0)
    total = jnp.broadcast_to(jnp.sum(total, axis=1, keepdims=True), (8, nz))
    dot = [total[i : i + 1, :] for i in range(8)]
    m = [dot[0], dot[1]]
    for k in range(2, 8):
        m.append(2.0 * dot[k] - m[k % 2])
    c0, c1, c2, c3 = cg_coefficients(m)

    def potential(x):
        phi_s[x + 1] = c0 * p0[x + H] + c1 * p1[x + H] + c2 * p2[x + H] + c3 * p3[x + H]

    sweep(-1, cx + 1, potential)

    sub_y = lax.broadcasted_iota(jnp.int32, (cy, nz), 0)
    lanes = lax.broadcasted_iota(jnp.int32, (cy, nz), 1)
    pull = DT * 0.5

    def advance(x):
        phi = phi_s[x + 1]
        u = us[x + 2] - pull * (phi_s[x + 2, 0:cy, :] - phi_s[x, 0:cy, :])
        v = vs[x] - pull * (north(phi) - south(phi))[:cy]
        phi = phi[:cy]
        w = le[x] - pull * (not_top * up(phi) - not_bot * down(phi))
        uo_ref[x] = u
        vo_ref[x] = v
        wo_ref[x] = w
        u_p, u_m = jnp.maximum(u, 0.0), jnp.minimum(u, 0.0)
        v_p, v_m = jnp.maximum(v, 0.0), jnp.minimum(v, 0.0)
        w_p, w_m = jnp.maximum(w, 0.0) * not_bot, jnp.minimum(w, 0.0) * not_top

        def move(f):
            tall = f[x + 1]
            h = tall[:cy]
            return h - DT * (
                u_p * (h - f[x, 0:cy, :])
                + u_m * (f[x + 2, 0:cy, :] - h)
                + v_p * (h - south(tall)[:cy])
                + v_m * (north(tall)[:cy] - h)
                + w_p * (h - down(h))
                + w_m * (up(h) - h)
            )

        tt, qq = move(te), move(qe)
        to_ref[x] = tt
        qo_ref[x] = qq
        sat = qq * jnp.exp(-CLAUSIUS_FACTOR * tt) - 1.0
        both = jnp.where(
            lanes < half, pltpu.roll(sat, nz - KLO, 1), pltpu.roll(tt, nz - KLO + half, 1)
        )
        odd = pltpu.roll(pltpu.roll(both, cy - 1, 0), nlev, 1)
        packed[x] = jnp.where(lanes % half < nlev, both, odd)

    sweep(0, cx, advance)
    for x in range(cx):
        for b in range(NBD):
            blk[b, x : x + 1, :] = packed[x, 2 * b : 2 * b + 1, :]

    f32 = jnp.float32
    left = lax.broadcasted_iota(jnp.int32, (cx, nz), 1) < half
    for r in range(nrow):
        o, t = r // slots, r % slots
        table = None
        for b in range(t, NBD, slots):
            term = jnp.where(map_s[0, b] == o, 1.0, 0.0) * blk[b]
            table = term if table is None else table + term
        big = table.astype(jnp.bfloat16).astype(f32)
        rest = table - big
        lhs = jnp.concatenate(
            [
                jnp.where(left, big, pltpu.roll(rest, half, 1)),
                jnp.where(left, pltpu.roll(big, half, 1), rest),
            ],
            axis=0,
        ).astype(jnp.bfloat16)
        res = jnp.dot(lhs, hot_s[r], preferred_element_type=f32)
        mask = narrow == col_s[r : r + 1, :]
        sat_s[r : r + 1, :] = jnp.sum(keep(mask, res[:cx]), axis=0, keepdims=True)
        tmp_s[r : r + 1, :] = jnp.sum(keep(mask, res[cx:]), axis=0, keepdims=True)

    rate = (2.0 * SUB_STEP * GROWTH) * jnp.exp(GROWTH_SLOPE * tmp_s[...])
    gain = rate * sat_s[...]
    loss = rate * CURVATURE
    old = size_d[...]
    new = old
    for _ in range(NSUB):
        new = jnp.maximum(new + gain - loss * lax.rsqrt(new), FLOOR_SQUARE)
    for o in range(ngx):
        xb[o] = new[o * slots : (o + 1) * slots]
    backs = []
    for o in range(1, ngx):
        peer = lax.rem(gx + o, ngx)
        backs.append(send(xb.at[peer], rb.at[gx], (grp, peer, gy)))
    rb[gx] = xb[gx]
    sat_s[...] = CONDENSE * mult_d[...] * (new * jnp.sqrt(new) - old * jnp.sqrt(old))

    across = (((1,), (1,)), ((), ()))
    for r in range(nrow):
        mass = sat_s[r : r + 1, :]
        big = mass.astype(jnp.bfloat16).astype(f32)
        mask = narrow == col_s[r : r + 1, :]
        both = jnp.concatenate([keep(mask, big), keep(mask, mass - big)], axis=0)
        res = lax.dot_general(
            both.astype(jnp.bfloat16), hot_s[r], across, preferred_element_type=f32
        )
        out2[r] = res[:cx] + res[cx:]

    for b in range(NBD):
        acc = None
        for o in range(ngx):
            term = jnp.where(map_s[0, b] == o, 1.0, 0.0) * out2[o * slots + b % slots]
            acc = term if acc is None else acc + term
        blk[b] = acc
    for x in range(cx):
        for b in range(NBD):
            line = blk[b, x : x + 1, :]
            grid_c[x, 2 * b : 2 * b + 1, :] = line
            grid_c[x, 2 * b + 1 : 2 * b + 2, :] = line
    even = sub_y % 2 == 0
    cloudy = (lanes >= KLO) & (lanes < KHI)

    def column(x):
        f = grid_c[x]
        f = jnp.where(even, pltpu.roll(f, KLO, 1), pltpu.roll(f, KLO - nlev, 1))
        f = keep(cloudy, f)
        to_ref[x] += PHASE_WARMING * f
        qo_ref[x] -= f

    sweep(0, cx, column, 4)
    for copy in backs:
        copy.wait_recv()
    for o in range(ngx):
        r = slice(o * slots, (o + 1) * slots)
        so_ref[r, :] = jnp.where(living(o), rb[o], size_v[r, :])
    pltpu.make_async_copy(got_x, got_x, sum_send).wait()
    drain()


def finish(*refs):
    sem = refs[-1]
    n = len(refs) // 2
    copies = [pltpu.make_async_copy(refs[i], refs[n + i], sem.at[i]) for i in range(n)]
    for copy in copies:
        copy.start()
    for copy in copies:
        copy.wait()


def on_device(ngrp, ngx, ngy, t, q, u, v, w, owner, count, size, mult, cell):
    cx, cy, nz = t.shape
    nrow, dpb = size.shape[2:]
    slots = nrow // ngx
    rows = cy + 8
    nt = cy // 8
    f32 = jnp.float32

    def buf(*shape):
        return pltpu.VMEM(shape, f32)

    ext = buf(cx + 2 * H, rows, nz)
    side = buf(cx + 2, rows, nz)
    grid = buf(cx, cy, nz)
    vec = buf(nrow, dpb)
    ivec = pltpu.VMEM((nrow, dpb), jnp.int32)
    tables = buf(nrow, cx, nz)
    nsem = 12 + 2 * (ngx - 1)
    nsum = ngrp * ngx * ngy - 1
    hbm = pl.BlockSpec(memory_space=pltpu.HBM)
    vm = pl.BlockSpec(memory_space=pltpu.VMEM)
    mid = pl.pallas_call(
        functools.partial(kernel, ngrp, ngx, ngy, slots),
        out_shape=(grid,) * 5 + (vec,),
        in_specs=[hbm] * 10,
        out_specs=(vm,) * 6,
        scratch_shapes=[
            buf(cx + 4, cy, nz), grid, grid, side, side, grid, ext, ext, ext, ext, side,
            vec, vec, ivec,
            pltpu.SMEM((1, NBD), jnp.int32), pltpu.SMEM((1, nrow), jnp.int32),
            buf(2, 5 * nt + 1, 8, nz), buf(2, 5 * nt + 1, 8, nz),
            buf(2, cx + 2, 8, nz), buf(2, cx + 2, 8, nz),
            buf(4, 2, 8, nz), buf(4, 2, 8, nz),
            buf(ngx, 3, slots, dpb), buf(ngx, 3, slots, dpb),
            buf(1, nz), buf(nsum, 1, nz),
            buf(NBD, cx, nz), grid, ivec, ivec, vec, vec, vec, vec,
            pltpu.VMEM((nrow, nz, dpb), jnp.bfloat16),
            buf(ngx, slots, dpb), buf(ngx, slots, dpb), tables, grid,
            pltpu.SemaphoreType.DMA((10,)),
            pltpu.SemaphoreType.DMA((nsem,)),
            pltpu.SemaphoreType.DMA((nsem,)),
            pltpu.SemaphoreType.DMA,
            pltpu.SemaphoreType.DMA,
        ],
        compiler_params=pltpu.CompilerParams(
            collective_id=0, has_side_effects=True, vmem_limit_bytes=24 * 2**20
        ),
        name="cloud_step",
    )(
        *(
            pltpu.with_memory_space_constraint(a, pltpu.HBM)
            for a in (
                t, q, u, v, w, owner.reshape(1, -1), count.reshape(1, -1),
                size[0, 0], mult[0, 0], cell[0, 0],
            )
        )
    )
    outs = pl.pallas_call(
        finish,
        out_shape=tuple(jax.ShapeDtypeStruct(a.shape, f32) for a in mid),
        in_specs=[vm] * 6,
        out_specs=(hbm,) * 6,
        scratch_shapes=[pltpu.SemaphoreType.DMA((6,))],
        compiler_params=pltpu.CompilerParams(vmem_limit_bytes=4 * 2**20),
        name="finish",
    )(*mid)
    return outs[:5] + (outs[5][None, None],)


def solution(mesh):
    grid = P(("grp", "gx"), "gy", None)
    drop = P(("grp", "gx"), "gy", None, None)
    return jax.shard_map(
        functools.partial(on_device, mesh.shape["grp"], mesh.shape["gx"], mesh.shape["gy"]),
        mesh=mesh,
        in_specs=(grid,) * 7 + (drop,) * 3,
        out_specs=(grid,) * 5 + (drop,),
        check_vma=False,
    )
```

```python
import functools

import jax
import jax.numpy as jnp
from jax import lax
from jax.experimental import pallas as pl
from jax.experimental.pallas import tpu as pltpu
from jax.sharding import PartitionSpec as P

NBD = 8
NSUB = 4
ITERS = 4
KLO = 48
KHI = 80

DT = 0.15
THERMAL_LIFT = 0.5
HUMID_LIFT = 0.3
HELMHOLTZ = 0.001
CLAUSIUS_FACTOR = 0.2
GROWTH = 0.5
GROWTH_SLOPE = 0.1
SUB_STEP = 0.25
CURVATURE = 0.05
FLOOR_SQUARE = 0.04
CONDENSE = 0.2
PHASE_WARMING = 2.5

H = 4
MESH = pl.DeviceIdType.MESH
KA, KM, KS, KD, KP, KV, KC = 8, 8, 30, 12, 13, 24, 8
def sweep(lo, hi, body, k=8):
    turns = (hi - lo) // k

    def turn(i, c):
        for j in range(k):
            body(lo + i * k + j)
        return c

    lax.fori_loop(0, turns, turn, 0)
    for x in range(lo + turns * k, hi):
        body(x)


def cg_coefficients(m):
    def inner(a, b):
        total = None
        for i, ai in enumerate(a):
            part = None
            for j, bj in enumerate(b):
                term = bj * (0.5 * (m[i + j] + m[abs(i - j)]))
                part = term if part is None else part + term
            part = ai * part
            total = part if total is None else total + part
        return total

    one = jnp.ones_like(m[0])
    zero = jnp.zeros_like(m[0])

    def apply(d):
        out = [zero] * (len(d) + 1)
        for i, di in enumerate(d):
            out[i] = out[i] + 6.0 * di
            if i == 0:
                out[1] = out[1] + 6.0 * di
            else:
                out[i + 1] = out[i + 1] + 3.0 * di
                out[i - 1] = out[i - 1] + 3.0 * di
        return out

    res, d, pot, rr = [one], [one], [], m[0]
    for it in range(ITERS):
        img = apply(d)
        alpha = rr / inner(d, img)
        pot = [
            alpha * d[i] + (pot[i] if i < len(pot) else 0.0) for i in range(len(d))
        ]
        if it + 1 == ITERS:
            break
        res = [(res[i] if i < len(res) else zero) - alpha * img[i] for i in range(len(img))]
        new = inner(res, res)
        beta = new / rr
        d = [res[i] + (beta * d[i] if i < len(d) else 0.0) for i in range(len(res))]
        rr = new
    return pot


def kernel(
    ngrp, ngx, ngy, slots,
    t_hbm, q_hbm, u_hbm, v_hbm, w_hbm, map_hbm, cnt_hbm, size_hbm, mult_hbm, cell_hbm,
    to_ref, qo_ref, uo_ref, vo_ref, wo_ref, so_ref,
    us, vs, ws, te, qe, le, p0, p1, p2, p3, phi_s, size_v, mult_v, cell_v, map_s, cnt_s,
    xs, xr, ys, yr, cs, cr, ds, dr, part, got_x,
    blk, packed, pos_s, col_s, size_d, mult_d, sat_s, tmp_s, hot_s, xb, rb, out2, grid_c,
    load_sem, send_sem, recv_sem, sum_send, sum_recv,
):
    cx, cy, nz = t_hbm.shape
    rows = cy + 8
    nt = cy // 8
    grp, gx, gy = lax.axis_index("grp"), lax.axis_index("gx"), lax.axis_index("gy")
    nx = ngrp * ngx
    xt = grp * ngx + gx
    everyone = nx * ngy

    def dev(dx, dy):
        other = lax.rem(xt + dx + nx, nx)
        return (lax.div(other, ngx), lax.rem(other, ngx), lax.rem(gy + dy + ngy, ngy))

    me = (grp * ngx + gx) * ngy + gy
    low_half = 2 * gx < ngx
    y_of = [lax.rem(gy + dy, ngy) for dy in range(ngy)]

    def visit(act):
        def turn_x(k, c):
            x = jnp.where(low_half, ngx - 1 - k, k)
            for dg in reversed(range(ngrp)):
                g = lax.rem(grp + dg, ngrp)
                for dy in reversed(range(ngy)):
                    if dg or dy:
                        act((g, x, y_of[dy]))
                    else:
                        pl.when(x != gx)(functools.partial(act, (g, x, y_of[dy])))
            return c

        lax.fori_loop(0, ngx, turn_x, 0)

    loads = []

    def fetch(src, dst):
        copy = pltpu.make_async_copy(src, dst, load_sem.at[len(loads)])
        copy.start()
        loads.append(copy)

    inside = (pl.ds(1, cx), pl.ds(0, cy))
    fetch(u_hbm, us.at[pl.ds(2, cx)])
    fetch(v_hbm, vs)
    fetch(w_hbm, ws)
    fetch(t_hbm, te.at[inside])
    fetch(q_hbm, qe.at[inside])

    barrier = pltpu.get_barrier_semaphore()

    def greet(target):
        pl.semaphore_signal(barrier, inc=1, device_id=target, device_id_type=MESH)

    visit(greet)
    fetch(cell_hbm, cell_v)
    fetch(size_hbm, size_v)
    fetch(mult_hbm, mult_v)
    fetch(cnt_hbm, cnt_s)
    fetch(map_hbm, map_s)

    lane = lax.broadcasted_iota(jnp.int32, (1, nz), 1)
    height = lane.astype(jnp.float32)
    rho = jnp.exp(-(height + 0.5) / nz)
    face = jnp.where(lane < nz - 1, jnp.exp(-(height + 1.0) / nz), 0.0)
    face_dn = jnp.where(lane > 0, jnp.exp(-height / nz), 0.0)
    not_top = jnp.where(lane < nz - 1, 1.0, 0.0)
    not_bot = jnp.where(lane > 0, 1.0, 0.0)
    rho_up = jnp.where(lane < nz - 1, jnp.exp(-(height + 1.5) / nz), 0.0)
    rho_dn = jnp.where(lane > 0, jnp.exp(-(height - 0.5) / nz), 0.0)
    half_r = -0.5 / DT
    rho_h, up_h, down_h = rho * half_r, rho_up * half_r, rho_dn * half_r
    sub = lax.broadcasted_iota(jnp.int32, (8, nz), 0)
    zero8 = jnp.zeros((8, nz), jnp.float32)

    def up(f):
        return pltpu.roll(f, nz - 1, 1)

    def down(f):
        return pltpu.roll(f, 1, 1)

    def north(f):
        return pltpu.roll(f, rows - 1, 0)

    def south(f):
        return pltpu.roll(f, 1, 0)

    def turn(f, s):
        return pltpu.roll(f, s, 0)

    def keep(mask, f):
        return jnp.where(mask, f, 0.0)

    def ends(f):
        return keep((sub == 0) | (sub == 7), f)

    for i in (0, 1, cx + 2, cx + 3):
        us[i] = jnp.zeros((cy, nz), jnp.float32)
    for copy in loads[:5]:
        copy.wait()

    def begin(x):
        tt, qq, vv = te[x + 1, 0:cy, :], qe[x + 1, 0:cy, :], vs[x]
        lift = ws[x] + DT * (THERMAL_LIFT * tt + HUMID_LIFT * qq)
        le[x] = lift
        tall = jnp.concatenate([vv, zero8], axis=0)
        c = rho_h * (north(tall) - south(tall))
        own = c[:cy] + (rho_h * (us[x + 3] - us[x + 1]) + (up_h * up(lift) - down_h * down(lift)))
        c0, c1, c2 = own[:8], own[cy - 8 :], c[cy:]
        p0[x + H, 0:cy, :] = own
        p0[x + H, cy:rows, :] = c2
        t0, t1, q0, q1 = tt[:8], tt[cy - 8 :], qq[:8], qq[cy - 8 :]
        ys[0, x + 1] = jnp.where(
            sub >= 4, c1, jnp.where(sub == 1, turn(t1, 2), jnp.where(sub == 2, turn(q1, 3), c2))
        )
        ys[1, x + 1] = jnp.where(
            sub < 4, c0, jnp.where(sub == 5, turn(t0, 5), jnp.where(sub == 6, turn(q0, 6), c2))
        )

    def rim(x):
        c = rho_h * (us[x + 3] - us[x + 1])
        p0[x + H, 0:cy, :] = c
        ys[0, x + 1] = keep(sub >= 4, c[cy - 8 :])
        ys[1, x + 1] = keep(sub < 4, c[:8])

    rim(-1)
    rim(cx)
    sweep(0, cx, begin, KA)

    for d, first, cols in ((0, cx - 4, (cx - 1, cx - 2, cx - 3)), (1, -1, (0, 1, 2))):
        for k in range(5):
            for i in range(nt):
                xs[d, k * nt + i] = p0[first + k + H, 8 * i : 8 * i + 8, :]
        a, b, c = (p0[x + H, cy:rows, :] for x in cols)
        xs[d, 5 * nt] = jnp.where(
            (sub == 0) | (sub == 7),
            a,
            jnp.where(
                (sub == 1) | (sub == 2), turn(b, 2), keep((sub == 3) | (sub == 4), turn(c, 4))
            ),
        )
    for d, side in ((0, 0), (1, 0), (2, 1), (3, 1)):
        y = [ys[side, cx - 3 + j if d in (0, 2) else 4 - j] for j in range(5)]
        if side == 0:
            cs[d, 0] = jnp.where(sub >= 4, y[4], turn(y[3], 3))
            cs[d, 1] = jnp.where(
                (sub == 0) | (sub >= 6),
                y[2],
                jnp.where(sub == 3, turn(y[0], 3), keep((sub == 1) | (sub == 2), turn(y[1], 2))),
            )
        else:
            cs[d, 0] = jnp.where(sub < 4, y[4], turn(y[3], 5))
            cs[d, 1] = jnp.where(
                (sub == 7) | (sub < 2),
                y[2],
                jnp.where(sub == 4, turn(y[0], 5), keep((sub == 2) | (sub == 3), turn(y[1], 3))),
            )

    pl.semaphore_wait(barrier, everyone - 1)

    started = []

    def send(src, dst, target):
        i = len(started)
        copy = pltpu.make_async_remote_copy(
            src_ref=src, dst_ref=dst, send_sem=send_sem.at[i], recv_sem=recv_sem.at[i],
            device_id=target, device_id_type=MESH,
        )
        copy.start()
        started.append(copy)
        return copy

    def drain():
        for copy in started[8:]:
            copy.wait_send()

    halo = [
        send(xs.at[0], xr.at[0], dev(1, 0)),
        send(xs.at[1], xr.at[1], dev(-1, 0)),
        send(cs.at[0], cr.at[0], dev(1, 1)),
        send(cs.at[1], cr.at[1], dev(-1, 1)),
        send(cs.at[2], cr.at[2], dev(1, -1)),
        send(cs.at[3], cr.at[3], dev(-1, -1)),
        send(ys.at[0], yr.at[0], dev(0, 1)),
        send(ys.at[1], yr.at[1], dev(0, -1)),
    ]
    for copy in loads[5:]:
        copy.wait()
    dpb = size_v.shape[1]
    nrow = ngx * slots
    place_of = lax.broadcasted_iota(jnp.int32, (slots, dpb), 1)
    slot_of = lax.broadcasted_iota(jnp.int32, (slots, dpb), 0)

    def living(o):
        limit = jnp.zeros((slots, dpb), jnp.int32)
        for t in range(slots):
            limit = jnp.where(slot_of == t, cnt_s[0, o * slots + t], limit)
        return place_of < limit

    for o in range(ngx):
        r = slice(o * slots, (o + 1) * slots)
        ds[o, 0] = size_v[r, :]
        ds[o, 1] = jnp.where(living(o), mult_v[r, :], 0.0)
        ds[o, 2] = cell_v[r, :].astype(jnp.float32)
    for copy in halo:
        copy.wait_send()
    sides = []
    for f in (te, qe):
        for edge, place, dx in ((cx, 0, 1), (1, cx + 1, -1)):
            sides.append(
                send(
                    f.at[pl.ds(edge, 1), pl.ds(0, cy)],
                    f.at[pl.ds(place, 1), pl.ds(0, cy)],
                    dev(dx, 0),
                )
            )

    moves = []
    for o in range(1, ngx):
        peer = lax.rem(gx + o, ngx)
        moves.append(send(ds.at[peer], dr.at[gx], (grp, peer, gy)))
    dr[gx] = ds[gx]

    for copy in halo:
        copy.wait_recv()


    def merge(x):
        a, b = yr[0, x + 1], yr[1, x + 1]
        p0[x + H, 0:8, :] += keep(sub == 0, a)
        p0[x + H, cy - 8 : cy, :] += keep(sub == 7, b)
        p0[x + H, cy:rows, :] += jnp.where(sub < 4, b, a)
        te[x + 1, cy:rows, :] = jnp.where(sub == 7, turn(a, 6), turn(b, 3))
        qe[x + 1, cy:rows, :] = jnp.where(sub == 7, turn(a, 5), turn(b, 2))

    sweep(0, cx, merge, KM)

    for d, ring in ((0, 0), (1, cx + 1)):
        a, b = cr[d, 0], cr[d, 1]
        low = [
            turn(b, 5),
            turn(b, 6),
            b,
            turn(a, 5),
            a,
        ]
        a, b = cr[2 + d, 0], cr[2 + d, 1]
        high = [
            turn(b, 3),
            turn(b, 5),
            b,
            turn(a, 3),
            a,
        ]
        misc = xr[d, 5 * nt]
        for j in range(5):
            x = j - 4 if d == 0 else cx + 3 - j
            k = j if d == 0 else 4 - j
            third = keep((sub >= 8 - j) & (sub >= 4), low[j]) + keep((sub < j) & (sub < 4), high[j])
            tiles = [xr[d, k * nt + i] for i in range(nt)]
            if j < 4:
                tiles[0] = tiles[0] + keep(sub == 0, low[j])
                tiles[nt - 1] = tiles[nt - 1] + keep(sub == 7, high[j])
            if j == 3:
                third = third + ends(misc) + jnp.where(sub < 4, yr[1, ring], yr[0, ring])
            elif j == 2:
                third = third + ends(turn(misc, 6))
            elif j == 1:
                third = third + ends(turn(misc, 4))
            for i in range(nt):
                s = slice(8 * i, 8 * i + 8)
                p0[x + H, s, :] = tiles[i] + p0[x + H, s, :] if j >= 3 else tiles[i]
            s = slice(cy, rows)
            p0[x + H, s, :] = third + p0[x + H, s, :] if j == 4 else third

    diag = ((4.0 + HELMHOLTZ) * rho + face + face_dn) / 6.0 - 1.0
    rho6, face6, face_dn6 = rho / 6.0, face / 6.0, face_dn / 6.0

    def scaled(f, x):
        c = f[x]
        side = f[x + 1] + f[x - 1] + north(c) + south(c)
        return diag * c - rho6 * side - face6 * up(c) - face_dn6 * down(c)

    def step1(x):
        p1[x] = scaled(p0, x)

    def step2(x):
        p2[x] = 2.0 * scaled(p1, x) - p0[x]

    def step3(x):
        p3[x] = 2.0 * scaled(p2, x) - p1[x]

    full = cx + 2 * H
    sweep(1, full - 1, step1, KS)
    sweep(2, full - 2, step2, KS)
    sweep(3, full - 3, step3, KS)

    def dots(x, acc):
        a0, a1, a2, a3 = p0[x, 0:cy, :], p1[x, 0:cy, :], p2[x, 0:cy, :], p3[x]
        a4 = 2.0 * scaled(p3, x)[:cy] - a2
        a3 = a3[:cy]
        pairs = ((a0, a0), (a0, a1), (a1, a1), (a1, a2), (a2, a2), (a2, a3), (a3, a3), (a3, a4))
        return tuple(s + f * g for s, (f, g) in zip(acc, pairs))

    def dots_some(i, acc):
        for j in range(KD):
            acc = dots(H + KD * i + j, acc)
        return acc

    acc = lax.fori_loop(0, cx // KD, dots_some, (jnp.zeros((cy, nz), jnp.float32),) * 8)
    for x in range(cx // KD * KD, cx):
        acc = dots(H + x, acc)
    corner = lax.broadcasted_iota(jnp.int32, (8, nz), 0) == lax.broadcasted_iota(
        jnp.int32, (8, nz), 1
    )
    sums = jnp.concatenate([jnp.sum(a, axis=0, keepdims=True) for a in acc], axis=0)
    sums = jnp.sum(sums, axis=1, keepdims=True)
    part[...] = jnp.sum(jnp.where(corner, sums, 0.0), axis=0, keepdims=True)
    got_x[me] = part[...]

    def share(target):
        pltpu.make_async_remote_copy(
            src_ref=part, dst_ref=got_x.at[me], send_sem=sum_send, recv_sem=sum_recv,
            device_id=target, device_id_type=MESH,
        ).start()

    visit(share)
    bulk = got_x.at[pl.ds(0, everyone - 1)]

    for copy in sides + moves:
        copy.wait_recv()
    half = nz // 2
    nlev = KHI - KLO
    for o in range(ngx):
        r = slice(o * slots, (o + 1) * slots)
        size_d[r, :] = dr[o, 0]
        mult_d[r, :] = dr[o, 1]
        cell = dr[o, 2].astype(jnp.int32)
        col_s[r, :] = cell // (2 * nz)
        pos_s[r, :] = (cell // nz) % 2 * nlev + cell % nz - KLO
    wide = lax.broadcasted_iota(jnp.int32, (half, dpb), 0)
    narrow = lax.broadcasted_iota(jnp.int32, (cx, dpb), 0)
    for r in range(nrow):
        one = jnp.where(wide == pos_s[r : r + 1, :], 1.0, 0.0).astype(jnp.bfloat16)
        hot_s[r, 0:half, :] = one
        hot_s[r, half:nz, :] = one

    pltpu.make_async_copy(bulk, bulk, sum_recv).wait()
    total = got_x[0]
    for o in range(1, everyone):
        total = total + got_x[o]
    total = jnp.where(corner, total, 0.0)
    total = jnp.broadcast_to(jnp.sum(total, axis=1, keepdims=True), (8, nz))
    dot = [total[i : i + 1, :] for i in range(8)]
    m = [dot[0], dot[1]]
    for k in range(2, 8):
        m.append(2.0 * dot[k] - m[k % 2])
    c0, c1, c2, c3 = cg_coefficients(m)

    def potential(x):
        phi_s[x + 1] = c0 * p0[x + H] + c1 * p1[x + H] + c2 * p2[x + H] + c3 * p3[x + H]

    sweep(-1, cx + 1, potential, KP)

    sub_y = lax.broadcasted_iota(jnp.int32, (cy, nz), 0)
    lanes = lax.broadcasted_iota(jnp.int32, (cy, nz), 1)
    pull = DT * 0.5

    def advance(x):
        phi = phi_s[x + 1]
        u = us[x + 2] - pull * (phi_s[x + 2, 0:cy, :] - phi_s[x, 0:cy, :])
        v = vs[x] - pull * (north(phi) - south(phi))[:cy]
        phi = phi[:cy]
        w = le[x] - pull * (not_top * up(phi) - not_bot * down(phi))
        uo_ref[x] = u
        vo_ref[x] = v
        wo_ref[x] = w
        u_p, u_m = jnp.maximum(u, 0.0), jnp.minimum(u, 0.0)
        v_p, v_m = jnp.maximum(v, 0.0), jnp.minimum(v, 0.0)
        w_p, w_m = jnp.maximum(w, 0.0) * not_bot, jnp.minimum(w, 0.0) * not_top

        def move(f):
            tall = f[x + 1]
            h = tall[:cy]
            return h - DT * (
                u_p * (h - f[x, 0:cy, :])
                + u_m * (f[x + 2, 0:cy, :] - h)
                + v_p * (h - south(tall)[:cy])
                + v_m * (north(tall)[:cy] - h)
                + w_p * (h - down(h))
                + w_m * (up(h) - h)
            )

        tt, qq = move(te), move(qe)
        to_ref[x] = tt
        qo_ref[x] = qq
        sat = qq * jnp.exp(-CLAUSIUS_FACTOR * tt) - 1.0
        both = jnp.where(
            lanes < half, pltpu.roll(sat, nz - KLO, 1), pltpu.roll(tt, nz - KLO + half, 1)
        )
        odd = pltpu.roll(pltpu.roll(both, cy - 1, 0), nlev, 1)
        packed[pl.ds(pl.multiple_of(x * cy, 8), cy), :] = jnp.where(lanes % half < nlev, both, odd)

    sweep(0, cx, advance, KV)
    for b in range(NBD):
        blk[b] = packed[pl.ds(2 * b, cx, stride=cy), :]

    f32 = jnp.float32
    left = lax.broadcasted_iota(jnp.int32, (cx, nz), 1) < half
    for r in range(nrow):
        o, t = r // slots, r % slots
        table = None
        for b in range(t, NBD, slots):
            term = jnp.where(map_s[0, b] == o, 1.0, 0.0) * blk[b]
            table = term if table is None else table + term
        big = table.astype(jnp.bfloat16).astype(f32)
        rest = table - big
        lhs = jnp.concatenate(
            [
                jnp.where(left, big, pltpu.roll(rest, half, 1)),
                jnp.where(left, pltpu.roll(big, half, 1), rest),
            ],
            axis=0,
        ).astype(jnp.bfloat16)
        res = jnp.dot(lhs, hot_s[r], preferred_element_type=f32)
        mask = narrow == col_s[r : r + 1, :]
        sat_s[r : r + 1, :] = jnp.sum(keep(mask, res[:cx]), axis=0, keepdims=True)
        tmp_s[r : r + 1, :] = jnp.sum(keep(mask, res[cx:]), axis=0, keepdims=True)

    rate = (2.0 * SUB_STEP * GROWTH) * jnp.exp(GROWTH_SLOPE * tmp_s[...])
    gain = rate * sat_s[...]
    loss = rate * CURVATURE
    old = size_d[...]
    new = old
    for _ in range(NSUB):
        new = jnp.maximum(new + gain - loss * lax.rsqrt(new), FLOOR_SQUARE)
    for o in range(ngx):
        xb[o] = new[o * slots : (o + 1) * slots]
    backs = []
    for o in range(1, ngx):
        peer = lax.rem(gx + o, ngx)
        backs.append(send(xb.at[peer], rb.at[gx], (grp, peer, gy)))
    rb[gx] = xb[gx]
    sat_s[...] = CONDENSE * mult_d[...] * (new * jnp.sqrt(new) - old * jnp.sqrt(old))

    across = (((1,), (1,)), ((), ()))
    for r in range(nrow):
        mass = sat_s[r : r + 1, :]
        big = mass.astype(jnp.bfloat16).astype(f32)
        mask = narrow == col_s[r : r + 1, :]
        both = jnp.concatenate([keep(mask, big), keep(mask, mass - big)], axis=0)
        res = lax.dot_general(
            both.astype(jnp.bfloat16), hot_s[r], across, preferred_element_type=f32
        )
        out2[r] = res[:cx] + res[cx:]

    for b in range(NBD):
        acc = None
        for o in range(ngx):
            term = jnp.where(map_s[0, b] == o, 1.0, 0.0) * out2[o * slots + b % slots]
            acc = term if acc is None else acc + term
        grid_c[pl.ds(2 * b, cx, stride=cy), :] = acc
        grid_c[pl.ds(2 * b + 1, cx, stride=cy), :] = acc
    even = sub_y % 2 == 0
    cloudy = (lanes >= KLO) & (lanes < KHI)

    def column(x):
        f = grid_c[pl.ds(pl.multiple_of(x * cy, 8), cy), :]
        f = jnp.where(even, pltpu.roll(f, KLO, 1), pltpu.roll(f, KLO - nlev, 1))
        f = keep(cloudy, f)
        to_ref[x] += PHASE_WARMING * f
        qo_ref[x] -= f

    sweep(0, cx, column, KC)
    for copy in backs:
        copy.wait_recv()
    for o in range(ngx):
        r = slice(o * slots, (o + 1) * slots)
        so_ref[r, :] = jnp.where(living(o), rb[o], size_v[r, :])
    pltpu.make_async_copy(bulk, bulk, sum_send).wait()
    drain()


def finish(*refs):
    sem = refs[-1]
    n = len(refs) // 2
    copies = [pltpu.make_async_copy(refs[i], refs[n + i], sem.at[i]) for i in range(n)]
    for copy in copies:
        copy.start()
    for copy in copies:
        copy.wait()


def on_device(ngrp, ngx, ngy, t, q, u, v, w, owner, count, size, mult, cell):
    cx, cy, nz = t.shape
    nrow, dpb = size.shape[2:]
    slots = nrow // ngx
    rows = cy + 8
    nt = cy // 8
    f32 = jnp.float32

    def buf(*shape):
        return pltpu.VMEM(shape, f32)

    ext = buf(cx + 2 * H, rows, nz)
    side = buf(cx + 2, rows, nz)
    grid = buf(cx, cy, nz)
    flat = buf(cx * cy, nz)
    vec = buf(nrow, dpb)
    ivec = pltpu.VMEM((nrow, dpb), jnp.int32)
    tables = buf(nrow, cx, nz)
    nsem = 12 + 2 * (ngx - 1)
    hbm = pl.BlockSpec(memory_space=pltpu.HBM)
    vm = pl.BlockSpec(memory_space=pltpu.VMEM)
    mid = pl.pallas_call(
        functools.partial(kernel, ngrp, ngx, ngy, slots),
        out_shape=(grid,) * 5 + (vec,),
        in_specs=[hbm] * 10,
        out_specs=(vm,) * 6,
        scratch_shapes=[
            buf(cx + 4, cy, nz), grid, grid, side, side, grid, ext, ext, ext, ext, side,
            vec, vec, ivec,
            pltpu.SMEM((1, NBD), jnp.int32), pltpu.SMEM((1, nrow), jnp.int32),
            buf(2, 5 * nt + 1, 8, nz), buf(2, 5 * nt + 1, 8, nz),
            buf(2, cx + 2, 8, nz), buf(2, cx + 2, 8, nz),
            buf(4, 2, 8, nz), buf(4, 2, 8, nz),
            buf(ngx, 3, slots, dpb), buf(ngx, 3, slots, dpb),
            buf(1, nz), buf(ngrp * ngx * ngy, 1, nz),
            buf(NBD, cx, nz), flat, ivec, ivec, vec, vec, vec, vec,
            pltpu.VMEM((nrow, nz, dpb), jnp.bfloat16),
            buf(ngx, slots, dpb), buf(ngx, slots, dpb), tables, flat,
            pltpu.SemaphoreType.DMA((10,)),
            pltpu.SemaphoreType.DMA((nsem,)),
            pltpu.SemaphoreType.DMA((nsem,)),
            pltpu.SemaphoreType.DMA,
            pltpu.SemaphoreType.DMA,
        ],
        compiler_params=pltpu.CompilerParams(
            collective_id=0, has_side_effects=True, vmem_limit_bytes=24 * 2**20
        ),
        name="cloud_step",
    )(
        *(
            pltpu.with_memory_space_constraint(a, pltpu.HBM)
            for a in (
                t, q, u, v, w, owner.reshape(1, -1), count.reshape(1, -1),
                size[0, 0], mult[0, 0], cell[0, 0],
            )
        )
    )
    outs = pl.pallas_call(
        finish,
        out_shape=tuple(jax.ShapeDtypeStruct(a.shape, f32) for a in mid),
        in_specs=[vm] * 6,
        out_specs=(hbm,) * 6,
        scratch_shapes=[pltpu.SemaphoreType.DMA((6,))],
        compiler_params=pltpu.CompilerParams(vmem_limit_bytes=4 * 2**20),
        name="finish",
    )(*mid)
    return outs[:5] + (outs[5][None, None],)


def solution(mesh):
    grid = P(("grp", "gx"), "gy", None)
    drop = P(("grp", "gx"), "gy", None, None)
    return jax.shard_map(
        functools.partial(on_device, mesh.shape["grp"], mesh.shape["gx"], mesh.shape["gy"]),
        mesh=mesh,
        in_specs=(grid,) * 7 + (drop,) * 3,
        out_specs=(grid,) * 5 + (drop,),
        check_vma=False,
    )
```

```python
import functools

import jax
import jax.numpy as jnp
from jax import lax
from jax.experimental import pallas as pl
from jax.experimental.pallas import tpu as pltpu
from jax.sharding import PartitionSpec as P

NBD = 8
NSUB = 4
ITERS = 4
KLO = 48
KHI = 80

DT = 0.15
THERMAL_LIFT = 0.5
HUMID_LIFT = 0.3
HELMHOLTZ = 0.001
CLAUSIUS_FACTOR = 0.2
GROWTH = 0.5
GROWTH_SLOPE = 0.1
SUB_STEP = 0.25
CURVATURE = 0.05
FLOOR_SQUARE = 0.04
CONDENSE = 0.2
PHASE_WARMING = 2.5

H = 4
MESH = pl.DeviceIdType.MESH
def sweep(lo, hi, body, k=8):
    turns = (hi - lo) // k

    def turn(i, c):
        for j in range(k):
            body(lo + i * k + j)
        return c

    lax.fori_loop(0, turns, turn, 0)
    for x in range(lo + turns * k, hi):
        body(x)


def cg_coefficients(m):
    def inner(a, b):
        total = None
        for i, ai in enumerate(a):
            part = None
            for j, bj in enumerate(b):
                term = bj * (0.5 * (m[i + j] + m[abs(i - j)]))
                part = term if part is None else part + term
            part = ai * part
            total = part if total is None else total + part
        return total

    one = jnp.ones_like(m[0])
    zero = jnp.zeros_like(m[0])

    def apply(d):
        out = [zero] * (len(d) + 1)
        for i, di in enumerate(d):
            out[i] = out[i] + 6.0 * di
            if i == 0:
                out[1] = out[1] + 6.0 * di
            else:
                out[i + 1] = out[i + 1] + 3.0 * di
                out[i - 1] = out[i - 1] + 3.0 * di
        return out

    res, d, pot, rr = [one], [one], [], m[0]
    for it in range(ITERS):
        img = apply(d)
        alpha = rr / inner(d, img)
        pot = [
            alpha * d[i] + (pot[i] if i < len(pot) else 0.0) for i in range(len(d))
        ]
        if it + 1 == ITERS:
            break
        res = [(res[i] if i < len(res) else zero) - alpha * img[i] for i in range(len(img))]
        new = inner(res, res)
        beta = new / rr
        d = [res[i] + (beta * d[i] if i < len(d) else 0.0) for i in range(len(res))]
        rr = new
    return pot


def kernel(
    ngrp, ngx, ngy, slots,
    t_hbm, q_hbm, u_hbm, v_hbm, w_hbm, map_hbm, cnt_hbm, size_hbm, mult_hbm, cell_hbm,
    to_ref, qo_ref, uo_ref, vo_ref, wo_ref, so_ref,
    us, vs, ws, te, qe, le, p0, p1, p2, p3, grad, slope, size_v, mult_v, cell_v, map_s, cnt_s,
    xs, xr, ys, yr, cs, cr, ds, dr, part, got_x,
    blk, packed, pos_s, col_s, size_d, mult_d, sat_s, tmp_s, hot_s, xb, rb, out2, grid_c,
    load_sem, send_sem, recv_sem, sum_send, sum_recv,
):
    cx, cy, nz = t_hbm.shape
    rows = cy + 8
    nt = cy // 8
    grp, gx, gy = lax.axis_index("grp"), lax.axis_index("gx"), lax.axis_index("gy")
    nx = ngrp * ngx
    xt = grp * ngx + gx
    everyone = nx * ngy

    def dev(dx, dy):
        other = lax.rem(xt + dx + nx, nx)
        return (lax.div(other, ngx), lax.rem(other, ngx), lax.rem(gy + dy + ngy, ngy))

    me = (grp * ngx + gx) * ngy + gy
    low_half = 2 * gx < ngx
    y_of = [lax.rem(gy + dy, ngy) for dy in range(ngy)]

    def visit(act):
        def turn_x(k, c):
            x = jnp.where(low_half, ngx - 1 - k, k)
            for dg in reversed(range(ngrp)):
                g = lax.rem(grp + dg, ngrp)
                for dy in reversed(range(ngy)):
                    if dg or dy:
                        act((g, x, y_of[dy]))
                    else:
                        pl.when(x != gx)(functools.partial(act, (g, x, y_of[dy])))
            return c

        lax.fori_loop(0, ngx, turn_x, 0)

    loads = []

    def fetch(src, dst):
        copy = pltpu.make_async_copy(src, dst, load_sem.at[len(loads)])
        copy.start()
        loads.append(copy)

    inside = (pl.ds(1, cx), pl.ds(0, cy))
    fetch(u_hbm, us.at[pl.ds(2, cx)])
    fetch(v_hbm, vs)
    fetch(w_hbm, ws)
    fetch(t_hbm, te.at[inside])
    fetch(q_hbm, qe.at[inside])

    barrier = pltpu.get_barrier_semaphore()

    def greet(target):
        pl.semaphore_signal(barrier, inc=1, device_id=target, device_id_type=MESH)

    visit(greet)
    fetch(cell_hbm, cell_v)
    fetch(size_hbm, size_v)
    fetch(mult_hbm, mult_v)
    fetch(cnt_hbm, cnt_s)
    fetch(map_hbm, map_s)

    lane = lax.broadcasted_iota(jnp.int32, (1, nz), 1)
    height = lane.astype(jnp.float32)
    rho = jnp.exp(-(height + 0.5) / nz)
    face = jnp.where(lane < nz - 1, jnp.exp(-(height + 1.0) / nz), 0.0)
    face_dn = jnp.where(lane > 0, jnp.exp(-height / nz), 0.0)
    not_top = jnp.where(lane < nz - 1, 1.0, 0.0)
    not_bot = jnp.where(lane > 0, 1.0, 0.0)
    rho_up = jnp.where(lane < nz - 1, jnp.exp(-(height + 1.5) / nz), 0.0)
    rho_dn = jnp.where(lane > 0, jnp.exp(-(height - 0.5) / nz), 0.0)
    half_r = -0.5 / DT
    rho_h, up_h, down_h = rho * half_r, rho_up * half_r, rho_dn * half_r
    sub = lax.broadcasted_iota(jnp.int32, (8, nz), 0)
    zero8 = jnp.zeros((8, nz), jnp.float32)

    def up(f):
        return pltpu.roll(f, nz - 1, 1)

    def down(f):
        return pltpu.roll(f, 1, 1)

    def north(f):
        return pltpu.roll(f, rows - 1, 0)

    def south(f):
        return pltpu.roll(f, 1, 0)

    def turn(f, s):
        return pltpu.roll(f, s, 0)

    def keep(mask, f):
        return jnp.where(mask, f, 0.0)

    def ends(f):
        return keep((sub == 0) | (sub == 7), f)

    for i in (0, 1, cx + 2, cx + 3):
        us[i] = jnp.zeros((cy, nz), jnp.float32)
    for copy in loads[:5]:
        copy.wait()

    def begin(x):
        tt, qq, vv = te[x + 1, 0:cy, :], qe[x + 1, 0:cy, :], vs[x]
        lift = ws[x] + DT * (THERMAL_LIFT * tt + HUMID_LIFT * qq)
        le[x] = lift
        tall = jnp.concatenate([vv, zero8], axis=0)
        c = rho_h * (north(tall) - south(tall))
        own = c[:cy] + (rho_h * (us[x + 3] - us[x + 1]) + (up_h * up(lift) - down_h * down(lift)))
        c0, c1, c2 = own[:8], own[cy - 8 :], c[cy:]
        p0[x + H, 0:cy, :] = own
        p0[x + H, cy:rows, :] = c2
        t0, t1, q0, q1 = tt[:8], tt[cy - 8 :], qq[:8], qq[cy - 8 :]
        ys[0, x + 1] = jnp.where(
            sub >= 4, c1, jnp.where(sub == 1, turn(t1, 2), jnp.where(sub == 2, turn(q1, 3), c2))
        )
        ys[1, x + 1] = jnp.where(
            sub < 4, c0, jnp.where(sub == 5, turn(t0, 5), jnp.where(sub == 6, turn(q0, 6), c2))
        )

    def rim(x):
        c = rho_h * (us[x + 3] - us[x + 1])
        p0[x + H, 0:cy, :] = c
        ys[0, x + 1] = keep(sub >= 4, c[cy - 8 :])
        ys[1, x + 1] = keep(sub < 4, c[:8])

    rim(-1)
    rim(cx)
    sweep(0, cx, begin, 8)

    for d, first, cols in ((0, cx - 4, (cx - 1, cx - 2, cx - 3)), (1, -1, (0, 1, 2))):
        for k in range(5):
            for i in range(nt):
                xs[d, k * nt + i] = p0[first + k + H, 8 * i : 8 * i + 8, :]
        a, b, c = (p0[x + H, cy:rows, :] for x in cols)
        xs[d, 5 * nt] = jnp.where(
            (sub == 0) | (sub == 7),
            a,
            jnp.where(
                (sub == 1) | (sub == 2), turn(b, 2), keep((sub == 3) | (sub == 4), turn(c, 4))
            ),
        )
    for d, side in ((0, 0), (1, 0), (2, 1), (3, 1)):
        y = [ys[side, cx - 3 + j if d in (0, 2) else 4 - j] for j in range(5)]
        if side == 0:
            cs[d, 0] = jnp.where(sub >= 4, y[4], turn(y[3], 3))
            cs[d, 1] = jnp.where(
                (sub == 0) | (sub >= 6),
                y[2],
                jnp.where(sub == 3, turn(y[0], 3), keep((sub == 1) | (sub == 2), turn(y[1], 2))),
            )
        else:
            cs[d, 0] = jnp.where(sub < 4, y[4], turn(y[3], 5))
            cs[d, 1] = jnp.where(
                (sub == 7) | (sub < 2),
                y[2],
                jnp.where(sub == 4, turn(y[0], 5), keep((sub == 2) | (sub == 3), turn(y[1], 3))),
            )

    pl.semaphore_wait(barrier, everyone - 1)

    started = []

    def send(src, dst, target):
        i = 8 + len(started)
        copy = pltpu.make_async_remote_copy(
            src_ref=src, dst_ref=dst, send_sem=send_sem.at[i], recv_sem=recv_sem.at[i],
            device_id=target, device_id_type=MESH,
        )
        copy.start()
        started.append(copy)
        return copy

    def drain():
        for copy in started:
            copy.wait_send()

    def halo_copy(i, src, dst, target):
        return pltpu.make_async_remote_copy(
            src_ref=src, dst_ref=dst, send_sem=send_sem.at[i], recv_sem=recv_sem.at[i],
            device_id=target, device_id_type=MESH,
        )

    def side_copies(d):
        step = 1 - 2 * d
        return [
            halo_copy(2 + d, cs.at[d], cr.at[d], dev(step, 1)),
            halo_copy(4 + d, cs.at[2 + d], cr.at[2 + d], dev(step, -1)),
            halo_copy(d, xs.at[d], xr.at[d], dev(step, 0)),
        ]

    def send_side(d):
        for copy in side_copies(d):
            copy.start()

    outer = jnp.where(low_half, 1, 0)
    rim_tile = (gx == 0) | (gx == ngx - 1)
    pl.when(rim_tile)(functools.partial(send_side, outer))
    row_copies = [
        halo_copy(6, ys.at[0], yr.at[0], dev(0, 1)),
        halo_copy(7, ys.at[1], yr.at[1], dev(0, -1)),
    ]
    for copy in row_copies:
        copy.start()
    halo = side_copies(0) + side_copies(1) + row_copies
    for copy in loads[5:]:
        copy.wait()
    dpb = size_v.shape[1]
    nrow = ngx * slots
    place_of = lax.broadcasted_iota(jnp.int32, (slots, dpb), 1)
    slot_of = lax.broadcasted_iota(jnp.int32, (slots, dpb), 0)

    def living(o):
        limit = jnp.zeros((slots, dpb), jnp.int32)
        for t in range(slots):
            limit = jnp.where(slot_of == t, cnt_s[0, o * slots + t], limit)
        return place_of < limit

    for o in range(ngx):
        r = slice(o * slots, (o + 1) * slots)
        ds[o, 0] = size_v[r, :]
        ds[o, 1] = jnp.where(living(o), mult_v[r, :], 0.0)
        ds[o, 2] = cell_v[r, :].astype(jnp.float32)
    pl.when(jnp.logical_not(rim_tile))(functools.partial(send_side, outer))
    send_side(1 - outer)
    for copy in halo:
        copy.wait_send()
    sides = []
    for f in (te, qe):
        for edge, place, dx in ((cx, 0, 1), (1, cx + 1, -1)):
            sides.append(
                send(
                    f.at[pl.ds(edge, 1), pl.ds(0, cy)],
                    f.at[pl.ds(place, 1), pl.ds(0, cy)],
                    dev(dx, 0),
                )
            )

    moves = []
    for o in range(1, ngx):
        peer = lax.rem(gx + o, ngx)
        moves.append(send(ds.at[peer], dr.at[gx], (grp, peer, gy)))
    dr[gx] = ds[gx]

    for copy in halo:
        copy.wait_recv()


    def merge(x):
        a, b = yr[0, x + 1], yr[1, x + 1]
        p0[x + H, 0:8, :] += keep(sub == 0, a)
        p0[x + H, cy - 8 : cy, :] += keep(sub == 7, b)
        p0[x + H, cy:rows, :] += jnp.where(sub < 4, b, a)
        te[x + 1, cy:rows, :] = jnp.where(sub == 7, turn(a, 6), turn(b, 3))
        qe[x + 1, cy:rows, :] = jnp.where(sub == 7, turn(a, 5), turn(b, 2))

    sweep(0, cx, merge, 8)

    for d, ring in ((0, 0), (1, cx + 1)):
        a, b = cr[d, 0], cr[d, 1]
        low = [
            turn(b, 5),
            turn(b, 6),
            b,
            turn(a, 5),
            a,
        ]
        a, b = cr[2 + d, 0], cr[2 + d, 1]
        high = [
            turn(b, 3),
            turn(b, 5),
            b,
            turn(a, 3),
            a,
        ]
        misc = xr[d, 5 * nt]
        for j in range(5):
            x = j - 4 if d == 0 else cx + 3 - j
            k = j if d == 0 else 4 - j
            third = keep((sub >= 8 - j) & (sub >= 4), low[j]) + keep((sub < j) & (sub < 4), high[j])
            tiles = [xr[d, k * nt + i] for i in range(nt)]
            if j < 4:
                tiles[0] = tiles[0] + keep(sub == 0, low[j])
                tiles[nt - 1] = tiles[nt - 1] + keep(sub == 7, high[j])
            if j == 3:
                third = third + ends(misc) + jnp.where(sub < 4, yr[1, ring], yr[0, ring])
            elif j == 2:
                third = third + ends(turn(misc, 6))
            elif j == 1:
                third = third + ends(turn(misc, 4))
            for i in range(nt):
                s = slice(8 * i, 8 * i + 8)
                p0[x + H, s, :] = tiles[i] + p0[x + H, s, :] if j >= 3 else tiles[i]
            s = slice(cy, rows)
            p0[x + H, s, :] = third + p0[x + H, s, :] if j == 4 else third

    diag = ((4.0 + HELMHOLTZ) * rho + face + face_dn) / 6.0 - 1.0
    rho6, face6, face_dn6 = rho / 6.0, face / 6.0, face_dn / 6.0

    def scaled(f, x):
        c = f[x]
        side = f[x + 1] + f[x - 1] + north(c) + south(c)
        return diag * c - rho6 * side - face6 * up(c) - face_dn6 * down(c)

    def step1(x):
        p1[x] = scaled(p0, x)

    def step2(x):
        p2[x] = 2.0 * scaled(p1, x) - p0[x]

    def step3(x):
        p3[x] = 2.0 * scaled(p2, x) - p1[x]

    full = cx + 2 * H
    sweep(1, full - 1, step1, 30)
    sweep(2, full - 2, step2, 30)
    sweep(3, full - 3, step3, 30)

    def dots(x, acc):
        a0, a1, a2, a3 = p0[x, 0:cy, :], p1[x, 0:cy, :], p2[x, 0:cy, :], p3[x]
        a4 = 2.0 * scaled(p3, x)[:cy] - a2
        a3 = a3[:cy]
        pairs = ((a0, a0), (a0, a1), (a1, a1), (a1, a2), (a2, a2), (a2, a3), (a3, a3), (a3, a4))
        return tuple(s + f * g for s, (f, g) in zip(acc, pairs))

    def dots_some(i, acc):
        for j in range(12):
            acc = dots(H + 12 * i + j, acc)
        return acc

    acc = lax.fori_loop(0, cx // 12, dots_some, (jnp.zeros((cy, nz), jnp.float32),) * 8)
    for x in range(cx // 12 * 12, cx):
        acc = dots(H + x, acc)
    corner = lax.broadcasted_iota(jnp.int32, (8, nz), 0) == lax.broadcasted_iota(
        jnp.int32, (8, nz), 1
    )
    sums = jnp.concatenate([jnp.sum(a, axis=0, keepdims=True) for a in acc], axis=0)
    sums = jnp.sum(sums, axis=1, keepdims=True)
    part[...] = jnp.sum(jnp.where(corner, sums, 0.0), axis=0, keepdims=True)
    got_x[me] = part[...]

    def share(target):
        pltpu.make_async_remote_copy(
            src_ref=part, dst_ref=got_x.at[me], send_sem=sum_send, recv_sem=sum_recv,
            device_id=target, device_id_type=MESH,
        ).start()

    visit(share)
    bulk = got_x.at[pl.ds(0, everyone - 1)]

    for copy in sides + moves:
        copy.wait_recv()
    half = nz // 2
    nlev = KHI - KLO
    for o in range(ngx):
        r = slice(o * slots, (o + 1) * slots)
        size_d[r, :] = dr[o, 0]
        mult_d[r, :] = dr[o, 1]
        cell = dr[o, 2].astype(jnp.int32)
        col_s[r, :] = cell // (2 * nz)
        pos_s[r, :] = (cell // nz) % 2 * nlev + cell % nz - KLO
    wide = lax.broadcasted_iota(jnp.int32, (half, dpb), 0)
    narrow = lax.broadcasted_iota(jnp.int32, (cx, dpb), 0)
    for r in range(nrow):
        one = jnp.where(wide == pos_s[r : r + 1, :], 1.0, 0.0).astype(jnp.bfloat16)
        hot_s[r, 0:half, :] = one
        hot_s[r, half:nz, :] = one

    pull = DT * 0.5

    def prepare(x):
        for i, p in enumerate((p0, p1, p2, p3)):
            tall = p[x + H]
            own = tall[:cy]
            grad[0, i, x] = pull * (p[x + H + 1, 0:cy, :] - p[x + H - 1, 0:cy, :])
            grad[1, i, x] = pull * (north(tall) - south(tall))[:cy]
            grad[2, i, x] = pull * (not_top * up(own) - not_bot * down(own))
        for k, f in enumerate((te, qe)):
            tall = f[x + 1]
            h = tall[:cy]
            slope[k, 0, x] = DT * (h - f[x, 0:cy, :])
            slope[k, 1, x] = DT * (f[x + 2, 0:cy, :] - h)
            slope[k, 2, x] = DT * (h - south(tall)[:cy])
            slope[k, 3, x] = DT * (north(tall)[:cy] - h)
            slope[k, 4, x] = DT * not_bot * (h - down(h))
            slope[k, 5, x] = DT * not_top * (up(h) - h)

    sweep(0, cx, prepare, 4)
    pltpu.make_async_copy(bulk, bulk, sum_recv).wait()
    total = got_x[0]
    for o in range(1, everyone):
        total = total + got_x[o]
    total = jnp.where(corner, total, 0.0)
    total = jnp.broadcast_to(jnp.sum(total, axis=1, keepdims=True), (8, nz))
    dot = [total[i : i + 1, :] for i in range(8)]
    m = [dot[0], dot[1]]
    for k in range(2, 8):
        m.append(2.0 * dot[k] - m[k % 2])
    c0, c1, c2, c3 = cg_coefficients(m)

    sub_y = lax.broadcasted_iota(jnp.int32, (cy, nz), 0)
    lanes = lax.broadcasted_iota(jnp.int32, (cy, nz), 1)
    even = sub_y % 2 == 0

    def advance(x):
        def wind(now, k):
            return now - (
                (c0 * grad[k, 0, x] + c1 * grad[k, 1, x]) + (c2 * grad[k, 2, x] + c3 * grad[k, 3, x])
            )

        u, v, w = wind(us[x + 2], 0), wind(vs[x], 1), wind(le[x], 2)
        uo_ref[x] = u
        vo_ref[x] = v
        wo_ref[x] = w
        u_in, v_in, w_in = u > 0.0, v > 0.0, w > 0.0

        def move(f, k):
            return f[x + 1, 0:cy, :] - (
                u * jnp.where(u_in, slope[k, 0, x], slope[k, 1, x])
                + v * jnp.where(v_in, slope[k, 2, x], slope[k, 3, x])
                + w * jnp.where(w_in, slope[k, 4, x], slope[k, 5, x])
            )

        tt, qq = move(te, 0), move(qe, 1)
        to_ref[x] = tt
        qo_ref[x] = qq
        sat = qq * jnp.exp(-CLAUSIUS_FACTOR * tt) - 1.0
        for i in range(nt):
            a, b = sat[8 * i : 8 * i + 8], tt[8 * i : 8 * i + 8]
            first_col = jnp.where(pair, a, turn(b, 1))
            second_col = jnp.where(pair, turn(a, 7), b)
            both = jnp.where(
                lane < nlev,
                pltpu.roll(first_col, nz - KLO, 1),
                pltpu.roll(second_col, nz - KLO + nlev, 1),
            )
            big = both.astype(jnp.bfloat16).astype(f32)
            packed[pl.ds(pl.multiple_of(x * cy + 8 * i, 8), 8), :] = jnp.where(
                lane < half, big, pltpu.roll(both - big, half, 1)
            )

    f32 = jnp.float32
    pair = sub % 2 == 0
    sweep(0, cx, advance, 24)
    for b in range(NBD):
        for k in range(2):
            blk[b, k * cx : (k + 1) * cx, :] = packed[pl.ds(2 * b + k, cx, stride=cy), :]

    for r in range(nrow):
        o, t = r // slots, r % slots
        table = None
        for b in range(t, NBD, slots):
            term = jnp.where(map_s[0, b] == o, 1.0, 0.0) * blk[b]
            table = term if table is None else table + term
        lhs = table.astype(jnp.bfloat16)
        res = jnp.dot(lhs, hot_s[r], preferred_element_type=f32)
        mask = narrow == col_s[r : r + 1, :]
        sat_s[r : r + 1, :] = jnp.sum(keep(mask, res[:cx]), axis=0, keepdims=True)
        tmp_s[r : r + 1, :] = jnp.sum(keep(mask, res[cx:]), axis=0, keepdims=True)

    rate = (2.0 * SUB_STEP * GROWTH) * jnp.exp(GROWTH_SLOPE * tmp_s[...])
    gain = rate * sat_s[...]
    loss = rate * CURVATURE
    old = size_d[...]
    new = old
    for _ in range(NSUB):
        new = jnp.maximum(new + gain - loss * lax.rsqrt(new), FLOOR_SQUARE)
    for o in range(ngx):
        xb[o] = new[o * slots : (o + 1) * slots]
    backs = []
    for o in range(1, ngx):
        peer = lax.rem(gx + o, ngx)
        backs.append(send(xb.at[peer], rb.at[gx], (grp, peer, gy)))
    rb[gx] = xb[gx]
    sat_s[...] = CONDENSE * mult_d[...] * (new * jnp.sqrt(new) - old * jnp.sqrt(old))

    across = (((1,), (1,)), ((), ()))
    for r in range(nrow):
        mass = sat_s[r : r + 1, :]
        big = mass.astype(jnp.bfloat16).astype(f32)
        mask = narrow == col_s[r : r + 1, :]
        both = jnp.concatenate([keep(mask, big), keep(mask, mass - big)], axis=0)
        res = lax.dot_general(
            both.astype(jnp.bfloat16), hot_s[r], across, preferred_element_type=f32
        )
        out2[r] = res[:cx] + res[cx:]

    for b in range(NBD):
        acc = None
        for o in range(ngx):
            term = jnp.where(map_s[0, b] == o, 1.0, 0.0) * out2[o * slots + b % slots]
            acc = term if acc is None else acc + term
        grid_c[pl.ds(2 * b, cx, stride=cy), :] = acc
        grid_c[pl.ds(2 * b + 1, cx, stride=cy), :] = acc
    cloudy = (lanes >= KLO) & (lanes < KHI)

    def column(x):
        f = grid_c[pl.ds(pl.multiple_of(x * cy, 8), cy), :]
        f = jnp.where(even, pltpu.roll(f, KLO, 1), pltpu.roll(f, KLO - nlev, 1))
        f = keep(cloudy, f)
        to_ref[x] += PHASE_WARMING * f
        qo_ref[x] -= f

    sweep(0, cx, column, 8)
    for copy in backs:
        copy.wait_recv()
    for o in range(ngx):
        r = slice(o * slots, (o + 1) * slots)
        so_ref[r, :] = jnp.where(living(o), rb[o], size_v[r, :])
    pltpu.make_async_copy(bulk, bulk, sum_send).wait()
    drain()


def finish(*refs):
    sem = refs[-1]
    n = len(refs) // 2
    copies = [pltpu.make_async_copy(refs[i], refs[n + i], sem.at[i]) for i in range(n)]
    for copy in copies:
        copy.start()
    for copy in copies:
        copy.wait()


def on_device(ngrp, ngx, ngy, t, q, u, v, w, owner, count, size, mult, cell):
    cx, cy, nz = t.shape
    nrow, dpb = size.shape[2:]
    slots = nrow // ngx
    rows = cy + 8
    nt = cy // 8
    f32 = jnp.float32

    def buf(*shape):
        return pltpu.VMEM(shape, f32)

    ext = buf(cx + 2 * H, rows, nz)
    side = buf(cx + 2, rows, nz)
    grid = buf(cx, cy, nz)
    flat = buf(cx * cy, nz)
    vec = buf(nrow, dpb)
    ivec = pltpu.VMEM((nrow, dpb), jnp.int32)
    tables = buf(nrow, cx, nz)
    nsem = 12 + 2 * (ngx - 1)
    hbm = pl.BlockSpec(memory_space=pltpu.HBM)
    vm = pl.BlockSpec(memory_space=pltpu.VMEM)
    mid = pl.pallas_call(
        functools.partial(kernel, ngrp, ngx, ngy, slots),
        out_shape=(grid,) * 5 + (vec,),
        in_specs=[hbm] * 10,
        out_specs=(vm,) * 6,
        scratch_shapes=[
            buf(cx + 4, cy, nz), grid, grid, side, side, grid, ext, ext, ext, ext,
            buf(3, 4, cx, cy, nz), buf(2, 6, cx, cy, nz),
            vec, vec, ivec,
            pltpu.SMEM((1, NBD), jnp.int32), pltpu.SMEM((1, nrow), jnp.int32),
            buf(2, 5 * nt + 1, 8, nz), buf(2, 5 * nt + 1, 8, nz),
            buf(2, cx + 2, 8, nz), buf(2, cx + 2, 8, nz),
            buf(4, 2, 8, nz), buf(4, 2, 8, nz),
            buf(ngx, 3, slots, dpb), buf(ngx, 3, slots, dpb),
            buf(1, nz), buf(ngrp * ngx * ngy, 1, nz),
            buf(NBD, 2 * cx, nz), flat, ivec, ivec, vec, vec, vec, vec,
            pltpu.VMEM((nrow, nz, dpb), jnp.bfloat16),
            buf(ngx, slots, dpb), buf(ngx, slots, dpb), tables, flat,
            pltpu.SemaphoreType.DMA((10,)),
            pltpu.SemaphoreType.DMA((nsem,)),
            pltpu.SemaphoreType.DMA((nsem,)),
            pltpu.SemaphoreType.DMA,
            pltpu.SemaphoreType.DMA,
        ],
        compiler_params=pltpu.CompilerParams(
            collective_id=0, has_side_effects=True, vmem_limit_bytes=24 * 2**20
        ),
        name="cloud_step",
    )(
        *(
            pltpu.with_memory_space_constraint(a, pltpu.HBM)
            for a in (
                t, q, u, v, w, owner.reshape(1, -1), count.reshape(1, -1),
                size[0, 0], mult[0, 0], cell[0, 0],
            )
        )
    )
    outs = pl.pallas_call(
        finish,
        out_shape=tuple(jax.ShapeDtypeStruct(a.shape, f32) for a in mid),
        in_specs=[vm] * 6,
        out_specs=(hbm,) * 6,
        scratch_shapes=[pltpu.SemaphoreType.DMA((6,))],
        compiler_params=pltpu.CompilerParams(vmem_limit_bytes=4 * 2**20),
        name="finish",
    )(*mid)
    return outs[:5] + (outs[5][None, None],)


def solution(mesh):
    grid = P(("grp", "gx"), "gy", None)
    drop = P(("grp", "gx"), "gy", None, None)
    return jax.shard_map(
        functools.partial(on_device, mesh.shape["grp"], mesh.shape["gx"], mesh.shape["gy"]),
        mesh=mesh,
        in_specs=(grid,) * 7 + (drop,) * 3,
        out_specs=(grid,) * 5 + (drop,),
        check_vma=False,
    )
```

```python
import functools

import jax
import jax.numpy as jnp
from jax import lax
from jax.experimental import pallas as pl
from jax.experimental.pallas import tpu as pltpu
from jax.sharding import PartitionSpec as P

NBD = 8
NSUB = 4
ITERS = 4
KLO = 48
KHI = 80

DT = 0.15
THERMAL_LIFT = 0.5
HUMID_LIFT = 0.3
HELMHOLTZ = 0.001
CLAUSIUS_FACTOR = 0.2
GROWTH = 0.5
GROWTH_SLOPE = 0.1
SUB_STEP = 0.25
CURVATURE = 0.05
FLOOR_SQUARE = 0.04
CONDENSE = 0.2
PHASE_WARMING = 2.5

H = 4
MESH = pl.DeviceIdType.MESH
def sweep(lo, hi, body, k=8):
    turns = (hi - lo) // k

    def turn(i, c):
        for j in range(k):
            body(lo + i * k + j)
        return c

    lax.fori_loop(0, turns, turn, 0)
    for x in range(lo + turns * k, hi):
        body(x)


def cg_coefficients(m):
    def inner(a, b):
        total = None
        for i, ai in enumerate(a):
            part = None
            for j, bj in enumerate(b):
                term = bj * (0.5 * (m[i + j] + m[abs(i - j)]))
                part = term if part is None else part + term
            part = ai * part
            total = part if total is None else total + part
        return total

    one = jnp.ones_like(m[0])
    zero = jnp.zeros_like(m[0])

    def apply(d):
        out = [zero] * (len(d) + 1)
        for i, di in enumerate(d):
            out[i] = out[i] + 6.0 * di
            if i == 0:
                out[1] = out[1] + 6.0 * di
            else:
                out[i + 1] = out[i + 1] + 3.0 * di
                out[i - 1] = out[i - 1] + 3.0 * di
        return out

    res, d, pot, rr = [one], [one], [], m[0]
    for it in range(ITERS):
        img = apply(d)
        alpha = rr / inner(d, img)
        pot = [
            alpha * d[i] + (pot[i] if i < len(pot) else 0.0) for i in range(len(d))
        ]
        if it + 1 == ITERS:
            break
        res = [(res[i] if i < len(res) else zero) - alpha * img[i] for i in range(len(img))]
        new = inner(res, res)
        beta = new / rr
        d = [res[i] + (beta * d[i] if i < len(d) else 0.0) for i in range(len(res))]
        rr = new
    return pot


def kernel(
    ngrp, ngx, ngy, slots,
    t_hbm, q_hbm, u_hbm, v_hbm, w_hbm, map_hbm, cnt_hbm, size_hbm, mult_hbm, cell_hbm,
    to_ref, qo_ref, uo_ref, vo_ref, wo_ref, so_ref,
    us, vs, ws, te, qe, le, p0, p1, p2, p3, grad, slope, size_v, mult_v, cell_v, map_s, cnt_s,
    xs, xr, ys, yr, cs, cr, ds, dr, part, got_x,
    blk, packed, pos_s, col_s, size_d, mult_d, sat_s, tmp_s, grown_s, hot_s, xb, rb, out2, grid_c,
    load_sem, send_sem, recv_sem, sum_send, sum_recv,
):
    cx, cy, nz = t_hbm.shape
    rows = cy + 8
    nt = cy // 8
    grp, gx, gy = lax.axis_index("grp"), lax.axis_index("gx"), lax.axis_index("gy")
    nx = ngrp * ngx
    xt = grp * ngx + gx
    everyone = nx * ngy

    def dev(dx, dy):
        other = lax.rem(xt + dx + nx, nx)
        return (lax.div(other, ngx), lax.rem(other, ngx), lax.rem(gy + dy + ngy, ngy))

    me = (grp * ngx + gx) * ngy + gy
    low_half = 2 * gx < ngx
    y_of = [lax.rem(gy + dy, ngy) for dy in range(ngy)]

    def visit(act):
        def turn_x(k, c):
            x = jnp.where(low_half, ngx - 1 - k, k)
            for dg in reversed(range(ngrp)):
                g = lax.rem(grp + dg, ngrp)
                for dy in reversed(range(ngy)):
                    if dg or dy:
                        act((g, x, y_of[dy]))
                    else:
                        pl.when(x != gx)(functools.partial(act, (g, x, y_of[dy])))
            return c

        lax.fori_loop(0, ngx, turn_x, 0)

    loads = []

    def fetch(src, dst):
        copy = pltpu.make_async_copy(src, dst, load_sem.at[len(loads)])
        copy.start()
        loads.append(copy)

    inside = (pl.ds(1, cx), pl.ds(0, cy))
    fetch(u_hbm, us.at[pl.ds(2, cx)])
    fetch(v_hbm, vs)
    fetch(w_hbm, ws)
    fetch(t_hbm, te.at[inside])
    fetch(q_hbm, qe.at[inside])

    barrier = pltpu.get_barrier_semaphore()

    def greet(target):
        pl.semaphore_signal(barrier, inc=1, device_id=target, device_id_type=MESH)

    visit(greet)
    fetch(cell_hbm, cell_v)
    fetch(size_hbm, size_v)
    fetch(mult_hbm, mult_v)
    fetch(cnt_hbm, cnt_s)
    fetch(map_hbm, map_s)

    lane = lax.broadcasted_iota(jnp.int32, (1, nz), 1)
    height = lane.astype(jnp.float32)
    rho = jnp.exp(-(height + 0.5) / nz)
    face = jnp.where(lane < nz - 1, jnp.exp(-(height + 1.0) / nz), 0.0)
    face_dn = jnp.where(lane > 0, jnp.exp(-height / nz), 0.0)
    not_top = jnp.where(lane < nz - 1, 1.0, 0.0)
    not_bot = jnp.where(lane > 0, 1.0, 0.0)
    rho_up = jnp.where(lane < nz - 1, jnp.exp(-(height + 1.5) / nz), 0.0)
    rho_dn = jnp.where(lane > 0, jnp.exp(-(height - 0.5) / nz), 0.0)
    half_r = -0.5 / DT
    rho_h, up_h, down_h = rho * half_r, rho_up * half_r, rho_dn * half_r
    sub = lax.broadcasted_iota(jnp.int32, (8, nz), 0)
    zero8 = jnp.zeros((8, nz), jnp.float32)

    def up(f):
        return pltpu.roll(f, nz - 1, 1)

    def down(f):
        return pltpu.roll(f, 1, 1)

    def north(f):
        return pltpu.roll(f, rows - 1, 0)

    def south(f):
        return pltpu.roll(f, 1, 0)

    def turn(f, s):
        return pltpu.roll(f, s, 0)

    def keep(mask, f):
        return jnp.where(mask, f, 0.0)

    def ends(f):
        return keep((sub == 0) | (sub == 7), f)

    for i in (0, 1, cx + 2, cx + 3):
        us[i] = jnp.zeros((cy, nz), jnp.float32)
    for copy in loads[:5]:
        copy.wait()

    def begin(x):
        tt, qq, vv = te[x + 1, 0:cy, :], qe[x + 1, 0:cy, :], vs[x]
        lift = ws[x] + DT * (THERMAL_LIFT * tt + HUMID_LIFT * qq)
        le[x] = lift
        tall = jnp.concatenate([vv, zero8], axis=0)
        c = rho_h * (north(tall) - south(tall))
        own = c[:cy] + (rho_h * (us[x + 3] - us[x + 1]) + (up_h * up(lift) - down_h * down(lift)))
        c0, c1, c2 = own[:8], own[cy - 8 :], c[cy:]
        p0[x + H, 0:cy, :] = own
        p0[x + H, cy:rows, :] = c2
        t0, t1, q0, q1 = tt[:8], tt[cy - 8 :], qq[:8], qq[cy - 8 :]
        ys[0, x + 1] = jnp.where(
            sub >= 4, c1, jnp.where(sub == 1, turn(t1, 2), jnp.where(sub == 2, turn(q1, 3), c2))
        )
        ys[1, x + 1] = jnp.where(
            sub < 4, c0, jnp.where(sub == 5, turn(t0, 5), jnp.where(sub == 6, turn(q0, 6), c2))
        )

    def rim(x):
        c = rho_h * (us[x + 3] - us[x + 1])
        p0[x + H, 0:cy, :] = c
        ys[0, x + 1] = keep(sub >= 4, c[cy - 8 :])
        ys[1, x + 1] = keep(sub < 4, c[:8])

    rim(-1)
    rim(cx)
    sweep(0, cx, begin, 8)

    for d, first, cols in ((0, cx - 4, (cx - 1, cx - 2, cx - 3)), (1, -1, (0, 1, 2))):
        for k in range(5):
            for i in range(nt):
                xs[d, k * nt + i] = p0[first + k + H, 8 * i : 8 * i + 8, :]
        a, b, c = (p0[x + H, cy:rows, :] for x in cols)
        xs[d, 5 * nt] = jnp.where(
            (sub == 0) | (sub == 7),
            a,
            jnp.where(
                (sub == 1) | (sub == 2), turn(b, 2), keep((sub == 3) | (sub == 4), turn(c, 4))
            ),
        )
    for d, side in ((0, 0), (1, 0), (2, 1), (3, 1)):
        y = [ys[side, cx - 3 + j if d in (0, 2) else 4 - j] for j in range(5)]
        if side == 0:
            cs[d, 0] = jnp.where(sub >= 4, y[4], turn(y[3], 3))
            cs[d, 1] = jnp.where(
                (sub == 0) | (sub >= 6),
                y[2],
                jnp.where(sub == 3, turn(y[0], 3), keep((sub == 1) | (sub == 2), turn(y[1], 2))),
            )
        else:
            cs[d, 0] = jnp.where(sub < 4, y[4], turn(y[3], 5))
            cs[d, 1] = jnp.where(
                (sub == 7) | (sub < 2),
                y[2],
                jnp.where(sub == 4, turn(y[0], 5), keep((sub == 2) | (sub == 3), turn(y[1], 3))),
            )

    pl.semaphore_wait(barrier, everyone - 1)

    started = []

    def send(src, dst, target):
        i = 8 + len(started)
        copy = pltpu.make_async_remote_copy(
            src_ref=src, dst_ref=dst, send_sem=send_sem.at[i], recv_sem=recv_sem.at[i],
            device_id=target, device_id_type=MESH,
        )
        copy.start()
        started.append(copy)
        return copy

    def drain():
        for copy in started:
            copy.wait_send()

    def halo_copy(i, src, dst, target):
        return pltpu.make_async_remote_copy(
            src_ref=src, dst_ref=dst, send_sem=send_sem.at[i], recv_sem=recv_sem.at[i],
            device_id=target, device_id_type=MESH,
        )

    def side_copies(d):
        step = 1 - 2 * d
        return [
            halo_copy(2 + d, cs.at[d], cr.at[d], dev(step, 1)),
            halo_copy(4 + d, cs.at[2 + d], cr.at[2 + d], dev(step, -1)),
            halo_copy(d, xs.at[d], xr.at[d], dev(step, 0)),
        ]

    def send_side(d):
        for copy in side_copies(d):
            copy.start()

    outer = jnp.where(low_half, 1, 0)
    rim_tile = (gx == 0) | (gx == ngx - 1)
    pl.when(rim_tile)(functools.partial(send_side, outer))
    row_copies = [
        halo_copy(6, ys.at[0], yr.at[0], dev(0, 1)),
        halo_copy(7, ys.at[1], yr.at[1], dev(0, -1)),
    ]
    for copy in row_copies:
        copy.start()
    halo = side_copies(0) + side_copies(1) + row_copies
    for copy in loads[5:]:
        copy.wait()
    dpb = size_v.shape[1]
    nrow = ngx * slots
    place_of = lax.broadcasted_iota(jnp.int32, (slots, dpb), 1)
    slot_of = lax.broadcasted_iota(jnp.int32, (slots, dpb), 0)

    def living(o):
        limit = jnp.zeros((slots, dpb), jnp.int32)
        for t in range(slots):
            limit = jnp.where(slot_of == t, cnt_s[0, o * slots + t], limit)
        return place_of < limit

    for o in range(ngx):
        r = slice(o * slots, (o + 1) * slots)
        ds[o, 0] = size_v[r, :]
        ds[o, 1] = jnp.where(living(o), mult_v[r, :], 0.0)
        ds[o, 2] = cell_v[r, :].astype(jnp.float32)
    pl.when(jnp.logical_not(rim_tile))(functools.partial(send_side, outer))
    send_side(1 - outer)
    for copy in halo:
        copy.wait_send()
    sides = []
    for f in (te, qe):
        for edge, place, dx in ((cx, 0, 1), (1, cx + 1, -1)):
            sides.append(
                send(
                    f.at[pl.ds(edge, 1), pl.ds(0, cy)],
                    f.at[pl.ds(place, 1), pl.ds(0, cy)],
                    dev(dx, 0),
                )
            )

    moves = []
    for o in range(1, ngx):
        peer = lax.rem(gx + o, ngx)
        moves.append(send(ds.at[peer], dr.at[gx], (grp, peer, gy)))
    dr[gx] = ds[gx]

    for copy in halo:
        copy.wait_recv()


    def merge(x):
        a, b = yr[0, x + 1], yr[1, x + 1]
        p0[x + H, 0:8, :] += keep(sub == 0, a)
        p0[x + H, cy - 8 : cy, :] += keep(sub == 7, b)
        p0[x + H, cy:rows, :] += jnp.where(sub < 4, b, a)
        te[x + 1, cy:rows, :] = jnp.where(sub == 7, turn(a, 6), turn(b, 3))
        qe[x + 1, cy:rows, :] = jnp.where(sub == 7, turn(a, 5), turn(b, 2))

    sweep(0, cx, merge, 8)

    for d, ring in ((0, 0), (1, cx + 1)):
        a, b = cr[d, 0], cr[d, 1]
        low = [
            turn(b, 5),
            turn(b, 6),
            b,
            turn(a, 5),
            a,
        ]
        a, b = cr[2 + d, 0], cr[2 + d, 1]
        high = [
            turn(b, 3),
            turn(b, 5),
            b,
            turn(a, 3),
            a,
        ]
        misc = xr[d, 5 * nt]
        for j in range(5):
            x = j - 4 if d == 0 else cx + 3 - j
            k = j if d == 0 else 4 - j
            third = keep((sub >= 8 - j) & (sub >= 4), low[j]) + keep((sub < j) & (sub < 4), high[j])
            tiles = [xr[d, k * nt + i] for i in range(nt)]
            if j < 4:
                tiles[0] = tiles[0] + keep(sub == 0, low[j])
                tiles[nt - 1] = tiles[nt - 1] + keep(sub == 7, high[j])
            if j == 3:
                third = third + ends(misc) + jnp.where(sub < 4, yr[1, ring], yr[0, ring])
            elif j == 2:
                third = third + ends(turn(misc, 6))
            elif j == 1:
                third = third + ends(turn(misc, 4))
            for i in range(nt):
                s = slice(8 * i, 8 * i + 8)
                p0[x + H, s, :] = tiles[i] + p0[x + H, s, :] if j >= 3 else tiles[i]
            s = slice(cy, rows)
            p0[x + H, s, :] = third + p0[x + H, s, :] if j == 4 else third

    diag = ((4.0 + HELMHOLTZ) * rho + face + face_dn) / 6.0 - 1.0
    rho6, face6, face_dn6 = rho / 6.0, face / 6.0, face_dn / 6.0

    def scaled(f, x):
        c = f[x]
        side = f[x + 1] + f[x - 1] + north(c) + south(c)
        return diag * c - rho6 * side - face6 * up(c) - face_dn6 * down(c)

    def step1(x):
        p1[x] = scaled(p0, x)

    def step2(x):
        p2[x] = 2.0 * scaled(p1, x) - p0[x]

    def step3(x):
        p3[x] = 2.0 * scaled(p2, x) - p1[x]

    full = cx + 2 * H
    sweep(1, full - 1, step1, 30)
    sweep(2, full - 2, step2, 30)
    sweep(3, full - 3, step3, 30)

    def dots(x, acc):
        a0, a1, a2, a3 = p0[x, 0:cy, :], p1[x, 0:cy, :], p2[x, 0:cy, :], p3[x]
        a4 = 2.0 * scaled(p3, x)[:cy] - a2
        a3 = a3[:cy]
        pairs = ((a0, a0), (a0, a1), (a1, a1), (a1, a2), (a2, a2), (a2, a3), (a3, a3), (a3, a4))
        return tuple(s + f * g for s, (f, g) in zip(acc, pairs))

    def dots_some(i, acc):
        for j in range(12):
            acc = dots(H + 12 * i + j, acc)
        return acc

    acc = lax.fori_loop(0, cx // 12, dots_some, (jnp.zeros((cy, nz), jnp.float32),) * 8)
    for x in range(cx // 12 * 12, cx):
        acc = dots(H + x, acc)
    corner = lax.broadcasted_iota(jnp.int32, (8, nz), 0) == lax.broadcasted_iota(
        jnp.int32, (8, nz), 1
    )
    sums = jnp.concatenate([jnp.sum(a, axis=0, keepdims=True) for a in acc], axis=0)
    sums = jnp.sum(sums, axis=1, keepdims=True)
    part[...] = jnp.sum(jnp.where(corner, sums, 0.0), axis=0, keepdims=True)
    got_x[me] = part[...]

    def share(target):
        pltpu.make_async_remote_copy(
            src_ref=part, dst_ref=got_x.at[me], send_sem=sum_send, recv_sem=sum_recv,
            device_id=target, device_id_type=MESH,
        ).start()

    visit(share)
    bulk = got_x.at[pl.ds(0, everyone - 1)]

    for copy in sides + moves:
        copy.wait_recv()
    half = nz // 2
    nlev = KHI - KLO
    for o in range(ngx):
        r = slice(o * slots, (o + 1) * slots)
        size_d[r, :] = dr[o, 0]
        mult_d[r, :] = dr[o, 1]
        cell = dr[o, 2].astype(jnp.int32)
        col_s[r, :] = cell // (2 * nz)
        pos_s[r, :] = (cell // nz) % 2 * nlev + cell % nz - KLO
    wide = lax.broadcasted_iota(jnp.int32, (half, dpb), 0)
    narrow = lax.broadcasted_iota(jnp.int32, (cx, dpb), 0)
    for r in range(nrow):
        one = jnp.where(wide == pos_s[r : r + 1, :], 1.0, 0.0).astype(jnp.bfloat16)
        hot_s[r, 0:half, :] = one
        hot_s[r, half:nz, :] = one

    pull = DT * 0.5

    def prepare(x):
        for i, p in enumerate((p0, p1, p2, p3)):
            tall = p[x + H]
            own = tall[:cy]
            grad[0, i, x] = pull * (p[x + H + 1, 0:cy, :] - p[x + H - 1, 0:cy, :])
            grad[1, i, x] = pull * (north(tall) - south(tall))[:cy]
            grad[2, i, x] = pull * (not_top * up(own) - not_bot * down(own))
        for k, f in enumerate((te, qe)):
            tall = f[x + 1]
            h = tall[:cy]
            slope[k, 0, x] = DT * (h - f[x, 0:cy, :])
            slope[k, 1, x] = DT * (f[x + 2, 0:cy, :] - h)
            slope[k, 2, x] = DT * (h - south(tall)[:cy])
            slope[k, 3, x] = DT * (north(tall)[:cy] - h)
            slope[k, 4, x] = DT * not_bot * (h - down(h))
            slope[k, 5, x] = DT * not_top * (up(h) - h)

    sweep(0, cx, prepare, 4)
    pltpu.make_async_copy(bulk, bulk, sum_recv).wait()
    total = got_x[0]
    for o in range(1, everyone):
        total = total + got_x[o]
    total = jnp.where(corner, total, 0.0)
    total = jnp.broadcast_to(jnp.sum(total, axis=1, keepdims=True), (8, nz))
    dot = [total[i : i + 1, :] for i in range(8)]
    m = [dot[0], dot[1]]
    for k in range(2, 8):
        m.append(2.0 * dot[k] - m[k % 2])
    c0, c1, c2, c3 = cg_coefficients(m)

    sub_y = lax.broadcasted_iota(jnp.int32, (cy, nz), 0)
    lanes = lax.broadcasted_iota(jnp.int32, (cy, nz), 1)
    even = sub_y % 2 == 0

    def advance(x):
        def wind(now, k):
            return now - (
                (c0 * grad[k, 0, x] + c1 * grad[k, 1, x]) + (c2 * grad[k, 2, x] + c3 * grad[k, 3, x])
            )

        u, v, w = wind(us[x + 2], 0), wind(vs[x], 1), wind(le[x], 2)
        uo_ref[x] = u
        vo_ref[x] = v
        wo_ref[x] = w
        u_in, v_in, w_in = u > 0.0, v > 0.0, w > 0.0

        def move(f, k):
            return f[x + 1, 0:cy, :] - (
                u * jnp.where(u_in, slope[k, 0, x], slope[k, 1, x])
                + v * jnp.where(v_in, slope[k, 2, x], slope[k, 3, x])
                + w * jnp.where(w_in, slope[k, 4, x], slope[k, 5, x])
            )

        tt, qq = move(te, 0), move(qe, 1)
        to_ref[x] = tt
        qo_ref[x] = qq
        sat = qq * jnp.exp(-CLAUSIUS_FACTOR * tt) - 1.0
        for i in range(nt):
            a, b = sat[8 * i : 8 * i + 8], tt[8 * i : 8 * i + 8]
            first_col = jnp.where(pair, a, turn(b, 1))
            second_col = jnp.where(pair, turn(a, 7), b)
            both = jnp.where(
                lane < nlev,
                pltpu.roll(first_col, nz - KLO, 1),
                pltpu.roll(second_col, nz - KLO + nlev, 1),
            )
            big = both.astype(jnp.bfloat16).astype(f32)
            packed[pl.ds(pl.multiple_of(x * cy + 8 * i, 8), 8), :] = jnp.where(
                lane < half, big, pltpu.roll(both - big, half, 1)
            )

    f32 = jnp.float32
    pair = sub % 2 == 0
    sweep(0, cx, advance, 24)
    for b in range(NBD):
        for k in range(2):
            blk[b, k * cx : (k + 1) * cx, :] = packed[pl.ds(2 * b + k, cx, stride=cy), :]

    first = 8 + len(started)

    def back(place, peer):
        return pltpu.make_async_remote_copy(
            src_ref=xb.at[peer], dst_ref=rb.at[gx],
            send_sem=send_sem.at[first + place], recv_sem=recv_sem.at[first + place],
            device_id=(grp, peer, gy), device_id_type=MESH,
        )

    def back_start(peer):
        back(lax.rem(peer - gx + ngx, ngx) - 1, peer).start()

    backs = [back(p, lax.rem(gx + p + 1, ngx)) for p in range(ngx - 1)]
    middle = ngx // 2
    for owners in (range(middle), range(middle, ngx)):
        span = slice(owners[0] * slots, (owners[-1] + 1) * slots)
        for r in range(span.start, span.stop):
            o, t = r // slots, r % slots
            table = None
            for b in range(t, NBD, slots):
                term = jnp.where(map_s[0, b] == o, 1.0, 0.0) * blk[b]
                table = term if table is None else table + term
            lhs = table.astype(jnp.bfloat16)
            res = jnp.dot(lhs, hot_s[r], preferred_element_type=f32)
            mask = narrow == col_s[r : r + 1, :]
            sat_s[r : r + 1, :] = jnp.sum(keep(mask, res[:cx]), axis=0, keepdims=True)
            tmp_s[r : r + 1, :] = jnp.sum(keep(mask, res[cx:]), axis=0, keepdims=True)
        rate = (2.0 * SUB_STEP * GROWTH) * jnp.exp(GROWTH_SLOPE * tmp_s[span, :])
        gain = rate * sat_s[span, :]
        loss = rate * CURVATURE
        new = size_d[span, :]
        for _ in range(NSUB):
            new = jnp.maximum(new + gain - loss * lax.rsqrt(new), FLOOR_SQUARE)
        grown_s[span, :] = new
        for peer in owners:
            k = (peer - owners[0]) * slots
            xb[peer] = new[k : k + slots]
        for peer in owners:
            pl.when(peer != gx)(functools.partial(back_start, peer))
    old, new = size_d[...], grown_s[...]
    rb[gx] = xb[gx]
    sat_s[...] = CONDENSE * mult_d[...] * (new * jnp.sqrt(new) - old * jnp.sqrt(old))

    across = (((1,), (1,)), ((), ()))
    for r in range(nrow):
        mass = sat_s[r : r + 1, :]
        big = mass.astype(jnp.bfloat16).astype(f32)
        mask = narrow == col_s[r : r + 1, :]
        both = jnp.concatenate([keep(mask, big), keep(mask, mass - big)], axis=0)
        res = lax.dot_general(
            both.astype(jnp.bfloat16), hot_s[r], across, preferred_element_type=f32
        )
        out2[r] = res[:cx] + res[cx:]

    for b in range(NBD):
        acc = None
        for o in range(ngx):
            term = jnp.where(map_s[0, b] == o, 1.0, 0.0) * out2[o * slots + b % slots]
            acc = term if acc is None else acc + term
        grid_c[pl.ds(2 * b, cx, stride=cy), :] = acc
        grid_c[pl.ds(2 * b + 1, cx, stride=cy), :] = acc
    cloudy = (lanes >= KLO) & (lanes < KHI)

    def column(x):
        f = grid_c[pl.ds(pl.multiple_of(x * cy, 8), cy), :]
        f = jnp.where(even, pltpu.roll(f, KLO, 1), pltpu.roll(f, KLO - nlev, 1))
        f = keep(cloudy, f)
        to_ref[x] += PHASE_WARMING * f
        qo_ref[x] -= f

    sweep(0, cx, column, 8)
    for copy in backs:
        copy.wait_recv()
    for o in range(ngx):
        r = slice(o * slots, (o + 1) * slots)
        so_ref[r, :] = jnp.where(living(o), rb[o], size_v[r, :])
    for copy in backs:
        copy.wait_send()
    pltpu.make_async_copy(bulk, bulk, sum_send).wait()
    drain()


def finish(*refs):
    sem = refs[-1]
    n = len(refs) // 2
    copies = [pltpu.make_async_copy(refs[i], refs[n + i], sem.at[i]) for i in range(n)]
    for copy in copies:
        copy.start()
    for copy in copies:
        copy.wait()


def on_device(ngrp, ngx, ngy, t, q, u, v, w, owner, count, size, mult, cell):
    cx, cy, nz = t.shape
    nrow, dpb = size.shape[2:]
    slots = nrow // ngx
    rows = cy + 8
    nt = cy // 8
    f32 = jnp.float32

    def buf(*shape):
        return pltpu.VMEM(shape, f32)

    ext = buf(cx + 2 * H, rows, nz)
    side = buf(cx + 2, rows, nz)
    grid = buf(cx, cy, nz)
    flat = buf(cx * cy, nz)
    vec = buf(nrow, dpb)
    ivec = pltpu.VMEM((nrow, dpb), jnp.int32)
    tables = buf(nrow, cx, nz)
    nsem = 12 + 2 * (ngx - 1)
    hbm = pl.BlockSpec(memory_space=pltpu.HBM)
    vm = pl.BlockSpec(memory_space=pltpu.VMEM)
    mid = pl.pallas_call(
        functools.partial(kernel, ngrp, ngx, ngy, slots),
        out_shape=(grid,) * 5 + (vec,),
        in_specs=[hbm] * 10,
        out_specs=(vm,) * 6,
        scratch_shapes=[
            buf(cx + 4, cy, nz), grid, grid, side, side, grid, ext, ext, ext, ext,
            buf(3, 4, cx, cy, nz), buf(2, 6, cx, cy, nz),
            vec, vec, ivec,
            pltpu.SMEM((1, NBD), jnp.int32), pltpu.SMEM((1, nrow), jnp.int32),
            buf(2, 5 * nt + 1, 8, nz), buf(2, 5 * nt + 1, 8, nz),
            buf(2, cx + 2, 8, nz), buf(2, cx + 2, 8, nz),
            buf(4, 2, 8, nz), buf(4, 2, 8, nz),
            buf(ngx, 3, slots, dpb), buf(ngx, 3, slots, dpb),
            buf(1, nz), buf(ngrp * ngx * ngy, 1, nz),
            buf(NBD, 2 * cx, nz), flat, ivec, ivec, vec, vec, vec, vec, vec,
            pltpu.VMEM((nrow, nz, dpb), jnp.bfloat16),
            buf(ngx, slots, dpb), buf(ngx, slots, dpb), tables, flat,
            pltpu.SemaphoreType.DMA((10,)),
            pltpu.SemaphoreType.DMA((nsem,)),
            pltpu.SemaphoreType.DMA((nsem,)),
            pltpu.SemaphoreType.DMA,
            pltpu.SemaphoreType.DMA,
        ],
        compiler_params=pltpu.CompilerParams(
            collective_id=0, has_side_effects=True, vmem_limit_bytes=24 * 2**20
        ),
        name="cloud_step",
    )(
        *(
            pltpu.with_memory_space_constraint(a, pltpu.HBM)
            for a in (
                t, q, u, v, w, owner.reshape(1, -1), count.reshape(1, -1),
                size[0, 0], mult[0, 0], cell[0, 0],
            )
        )
    )
    outs = pl.pallas_call(
        finish,
        out_shape=tuple(jax.ShapeDtypeStruct(a.shape, f32) for a in mid),
        in_specs=[vm] * 6,
        out_specs=(hbm,) * 6,
        scratch_shapes=[pltpu.SemaphoreType.DMA((6,))],
        compiler_params=pltpu.CompilerParams(vmem_limit_bytes=4 * 2**20),
        name="finish",
    )(*mid)
    return outs[:5] + (outs[5][None, None],)


def solution(mesh):
    grid = P(("grp", "gx"), "gy", None)
    drop = P(("grp", "gx"), "gy", None, None)
    return jax.shard_map(
        functools.partial(on_device, mesh.shape["grp"], mesh.shape["gx"], mesh.shape["gy"]),
        mesh=mesh,
        in_specs=(grid,) * 7 + (drop,) * 3,
        out_specs=(grid,) * 5 + (drop,),
        check_vma=False,
    )
```

```python
import functools

import jax
import jax.numpy as jnp
from jax import lax
from jax.experimental import pallas as pl
from jax.experimental.pallas import tpu as pltpu
from jax.sharding import PartitionSpec as P

NBD = 8
NSUB = 4
ITERS = 4
KLO = 48
KHI = 80

DT = 0.15
THERMAL_LIFT = 0.5
HUMID_LIFT = 0.3
HELMHOLTZ = 0.001
CLAUSIUS_FACTOR = 0.2
GROWTH = 0.5
GROWTH_SLOPE = 0.1
SUB_STEP = 0.25
CURVATURE = 0.05
FLOOR_SQUARE = 0.04
CONDENSE = 0.2
PHASE_WARMING = 2.5

H = 4
MESH = pl.DeviceIdType.MESH
def sweep(lo, hi, body, k=8):
    turns = (hi - lo) // k

    def turn(i, c):
        for j in range(k):
            body(lo + i * k + j)
        return c

    lax.fori_loop(0, turns, turn, 0)
    for x in range(lo + turns * k, hi):
        body(x)


def cg_coefficients(m):
    def inner(a, b):
        total = None
        for i, ai in enumerate(a):
            part = None
            for j, bj in enumerate(b):
                term = bj * (0.5 * (m[i + j] + m[abs(i - j)]))
                part = term if part is None else part + term
            part = ai * part
            total = part if total is None else total + part
        return total

    one = jnp.ones_like(m[0])
    zero = jnp.zeros_like(m[0])

    def apply(d):
        out = [zero] * (len(d) + 1)
        for i, di in enumerate(d):
            out[i] = out[i] + 6.0 * di
            if i == 0:
                out[1] = out[1] + 6.0 * di
            else:
                out[i + 1] = out[i + 1] + 3.0 * di
                out[i - 1] = out[i - 1] + 3.0 * di
        return out

    res, d, pot, rr = [one], [one], [], m[0]
    for it in range(ITERS):
        img = apply(d)
        alpha = rr / inner(d, img)
        pot = [
            alpha * d[i] + (pot[i] if i < len(pot) else 0.0) for i in range(len(d))
        ]
        if it + 1 == ITERS:
            break
        res = [(res[i] if i < len(res) else zero) - alpha * img[i] for i in range(len(img))]
        new = inner(res, res)
        beta = new / rr
        d = [res[i] + (beta * d[i] if i < len(d) else 0.0) for i in range(len(res))]
        rr = new
    return pot


def kernel(
    ngrp, ngx, ngy, slots,
    t_hbm, q_hbm, u_hbm, v_hbm, w_hbm, map_hbm, cnt_hbm, size_hbm, mult_hbm, cell_hbm,
    to_ref, qo_ref, uo_ref, vo_ref, wo_ref, so_ref,
    us, vs, ws, te, qe, le, p0, p1, p2, p3, grad, slope, size_v, mult_v, cell_v, map_s, cnt_s,
    xs, xr, ys, yr, cs, cr, ds, dr, part, got_x,
    blk, packed, pos_s, col_s, size_d, mult_d, sat_s, tmp_s, grown_s, hot_s, xb, rb, out2, grid_c,
    load_sem, send_sem, recv_sem, sum_send, sum_recv,
):
    cx, cy, nz = t_hbm.shape
    rows = cy + 8
    nt = cy // 8
    grp, gx, gy = lax.axis_index("grp"), lax.axis_index("gx"), lax.axis_index("gy")
    nx = ngrp * ngx
    xt = grp * ngx + gx
    everyone = nx * ngy

    def dev(dx, dy):
        other = lax.rem(xt + dx + nx, nx)
        return (lax.div(other, ngx), lax.rem(other, ngx), lax.rem(gy + dy + ngy, ngy))

    me = (grp * ngx + gx) * ngy + gy
    low_half = 2 * gx < ngx
    y_of = [lax.rem(gy + dy, ngy) for dy in range(ngy)]

    def visit(act):
        def turn_x(k, c):
            x = jnp.where(low_half, ngx - 1 - k, k)
            for dg in reversed(range(ngrp)):
                g = lax.rem(grp + dg, ngrp)
                for dy in reversed(range(ngy)):
                    if dg or dy:
                        act((g, x, y_of[dy]))
                    else:
                        pl.when(x != gx)(functools.partial(act, (g, x, y_of[dy])))
            return c

        lax.fori_loop(0, ngx, turn_x, 0)

    loads = []

    def fetch(src, dst):
        copy = pltpu.make_async_copy(src, dst, load_sem.at[len(loads)])
        copy.start()
        loads.append(copy)

    inside = (pl.ds(1, cx), pl.ds(0, cy))
    fetch(u_hbm, us.at[pl.ds(2, cx)])
    fetch(v_hbm, vs)
    fetch(w_hbm, ws)
    fetch(t_hbm, te.at[inside])
    fetch(q_hbm, qe.at[inside])

    barrier = pltpu.get_barrier_semaphore()

    def greet(target):
        pl.semaphore_signal(barrier, inc=1, device_id=target, device_id_type=MESH)

    visit(greet)
    fetch(cell_hbm, cell_v)
    fetch(size_hbm, size_v)
    fetch(mult_hbm, mult_v)
    fetch(cnt_hbm, cnt_s)
    fetch(map_hbm, map_s)

    lane = lax.broadcasted_iota(jnp.int32, (1, nz), 1)
    height = lane.astype(jnp.float32)
    rho = jnp.exp(-(height + 0.5) / nz)
    face = jnp.where(lane < nz - 1, jnp.exp(-(height + 1.0) / nz), 0.0)
    face_dn = jnp.where(lane > 0, jnp.exp(-height / nz), 0.0)
    not_top = jnp.where(lane < nz - 1, 1.0, 0.0)
    not_bot = jnp.where(lane > 0, 1.0, 0.0)
    rho_up = jnp.where(lane < nz - 1, jnp.exp(-(height + 1.5) / nz), 0.0)
    rho_dn = jnp.where(lane > 0, jnp.exp(-(height - 0.5) / nz), 0.0)
    half_r = -0.5 / DT
    rho_h, up_h, down_h = rho * half_r, rho_up * half_r, rho_dn * half_r
    sub = lax.broadcasted_iota(jnp.int32, (8, nz), 0)
    zero8 = jnp.zeros((8, nz), jnp.float32)

    def up(f):
        return pltpu.roll(f, nz - 1, 1)

    def down(f):
        return pltpu.roll(f, 1, 1)

    def north(f):
        return pltpu.roll(f, rows - 1, 0)

    def south(f):
        return pltpu.roll(f, 1, 0)

    def turn(f, s):
        return pltpu.roll(f, s, 0)

    def keep(mask, f):
        return jnp.where(mask, f, 0.0)

    def ends(f):
        return keep((sub == 0) | (sub == 7), f)

    for i in (0, 1, cx + 2, cx + 3):
        us[i] = jnp.zeros((cy, nz), jnp.float32)
    for copy in loads[:5]:
        copy.wait()

    def begin(x):
        tt, qq, vv = te[x + 1, 0:cy, :], qe[x + 1, 0:cy, :], vs[x]
        lift = ws[x] + DT * (THERMAL_LIFT * tt + HUMID_LIFT * qq)
        le[x] = lift
        tall = jnp.concatenate([vv, zero8], axis=0)
        c = rho_h * (north(tall) - south(tall))
        own = c[:cy] + (rho_h * (us[x + 3] - us[x + 1]) + (up_h * up(lift) - down_h * down(lift)))
        c0, c1, c2 = own[:8], own[cy - 8 :], c[cy:]
        p0[x + H, 0:cy, :] = own
        p0[x + H, cy:rows, :] = c2
        t0, t1, q0, q1 = tt[:8], tt[cy - 8 :], qq[:8], qq[cy - 8 :]
        ys[0, x + 1] = jnp.where(
            sub >= 4, c1, jnp.where(sub == 1, turn(t1, 2), jnp.where(sub == 2, turn(q1, 3), c2))
        )
        ys[1, x + 1] = jnp.where(
            sub < 4, c0, jnp.where(sub == 5, turn(t0, 5), jnp.where(sub == 6, turn(q0, 6), c2))
        )

    def rim(x):
        c = rho_h * (us[x + 3] - us[x + 1])
        p0[x + H, 0:cy, :] = c
        ys[0, x + 1] = keep(sub >= 4, c[cy - 8 :])
        ys[1, x + 1] = keep(sub < 4, c[:8])

    rim(-1)
    rim(cx)
    sweep(0, cx, begin, 8)

    for d, first, cols in ((0, cx - 4, (cx - 1, cx - 2, cx - 3)), (1, -1, (0, 1, 2))):
        for k in range(5):
            for i in range(nt):
                xs[d, k * nt + i] = p0[first + k + H, 8 * i : 8 * i + 8, :]
        a, b, c = (p0[x + H, cy:rows, :] for x in cols)
        xs[d, 5 * nt] = jnp.where(
            (sub == 0) | (sub == 7),
            a,
            jnp.where(
                (sub == 1) | (sub == 2), turn(b, 2), keep((sub == 3) | (sub == 4), turn(c, 4))
            ),
        )
    for d, side in ((0, 0), (1, 0), (2, 1), (3, 1)):
        y = [ys[side, cx - 3 + j if d in (0, 2) else 4 - j] for j in range(5)]
        if side == 0:
            cs[d, 0] = jnp.where(sub >= 4, y[4], turn(y[3], 3))
            cs[d, 1] = jnp.where(
                (sub == 0) | (sub >= 6),
                y[2],
                jnp.where(sub == 3, turn(y[0], 3), keep((sub == 1) | (sub == 2), turn(y[1], 2))),
            )
        else:
            cs[d, 0] = jnp.where(sub < 4, y[4], turn(y[3], 5))
            cs[d, 1] = jnp.where(
                (sub == 7) | (sub < 2),
                y[2],
                jnp.where(sub == 4, turn(y[0], 5), keep((sub == 2) | (sub == 3), turn(y[1], 3))),
            )

    pl.semaphore_wait(barrier, everyone - 1)

    started = []

    def send(src, dst, target):
        i = 8 + len(started)
        copy = pltpu.make_async_remote_copy(
            src_ref=src, dst_ref=dst, send_sem=send_sem.at[i], recv_sem=recv_sem.at[i],
            device_id=target, device_id_type=MESH,
        )
        copy.start()
        started.append(copy)
        return copy

    def drain():
        for copy in started + halo[:6]:
            copy.wait_send()

    def halo_copy(i, src, dst, target):
        return pltpu.make_async_remote_copy(
            src_ref=src, dst_ref=dst, send_sem=send_sem.at[i], recv_sem=recv_sem.at[i],
            device_id=target, device_id_type=MESH,
        )

    def side_copies(d):
        step = 1 - 2 * d
        return [
            halo_copy(2 + d, cs.at[d], cr.at[d], dev(step, 1)),
            halo_copy(4 + d, cs.at[2 + d], cr.at[2 + d], dev(step, -1)),
            halo_copy(d, xs.at[d], xr.at[d], dev(step, 0)),
        ]

    def send_side(d):
        for copy in side_copies(d):
            copy.start()

    outer = jnp.where(low_half, 1, 0)
    rim_tile = (gx == 0) | (gx == ngx - 1)
    pl.when(rim_tile)(functools.partial(send_side, outer))
    row_copies = [
        halo_copy(6, ys.at[0], yr.at[0], dev(0, 1)),
        halo_copy(7, ys.at[1], yr.at[1], dev(0, -1)),
    ]
    for copy in row_copies:
        copy.start()
    halo = side_copies(0) + side_copies(1) + row_copies
    for copy in loads[5:]:
        copy.wait()
    dpb = size_v.shape[1]
    nrow = ngx * slots
    place_of = lax.broadcasted_iota(jnp.int32, (slots, dpb), 1)
    slot_of = lax.broadcasted_iota(jnp.int32, (slots, dpb), 0)

    def living(o):
        limit = jnp.zeros((slots, dpb), jnp.int32)
        for t in range(slots):
            limit = jnp.where(slot_of == t, cnt_s[0, o * slots + t], limit)
        return place_of < limit

    for o in range(ngx):
        r = slice(o * slots, (o + 1) * slots)
        ds[o, 0] = size_v[r, :]
        ds[o, 1] = jnp.where(living(o), mult_v[r, :], 0.0)
        ds[o, 2] = cell_v[r, :].astype(jnp.float32)
    pl.when(jnp.logical_not(rim_tile))(functools.partial(send_side, outer))
    send_side(1 - outer)
    for copy in row_copies:
        copy.wait_send()
    sides = []
    for f in (te, qe):
        for edge, place, dx in ((cx, 0, 1), (1, cx + 1, -1)):
            sides.append(
                send(
                    f.at[pl.ds(edge, 1), pl.ds(0, cy)],
                    f.at[pl.ds(place, 1), pl.ds(0, cy)],
                    dev(dx, 0),
                )
            )

    moves = []
    for o in range(1, ngx):
        peer = lax.rem(gx + o, ngx)
        moves.append(send(ds.at[peer], dr.at[gx], (grp, peer, gy)))
    dr[gx] = ds[gx]

    for copy in halo:
        copy.wait_recv()


    def merge(x):
        a, b = yr[0, x + 1], yr[1, x + 1]
        p0[x + H, 0:8, :] += keep(sub == 0, a)
        p0[x + H, cy - 8 : cy, :] += keep(sub == 7, b)
        p0[x + H, cy:rows, :] += jnp.where(sub < 4, b, a)
        te[x + 1, cy:rows, :] = jnp.where(sub == 7, turn(a, 6), turn(b, 3))
        qe[x + 1, cy:rows, :] = jnp.where(sub == 7, turn(a, 5), turn(b, 2))

    sweep(0, cx, merge, 8)

    for d, ring in ((0, 0), (1, cx + 1)):
        a, b = cr[d, 0], cr[d, 1]
        low = [
            turn(b, 5),
            turn(b, 6),
            b,
            turn(a, 5),
            a,
        ]
        a, b = cr[2 + d, 0], cr[2 + d, 1]
        high = [
            turn(b, 3),
            turn(b, 5),
            b,
            turn(a, 3),
            a,
        ]
        misc = xr[d, 5 * nt]
        for j in range(5):
            x = j - 4 if d == 0 else cx + 3 - j
            k = j if d == 0 else 4 - j
            third = keep((sub >= 8 - j) & (sub >= 4), low[j]) + keep((sub < j) & (sub < 4), high[j])
            tiles = [xr[d, k * nt + i] for i in range(nt)]
            if j < 4:
                tiles[0] = tiles[0] + keep(sub == 0, low[j])
                tiles[nt - 1] = tiles[nt - 1] + keep(sub == 7, high[j])
            if j == 3:
                third = third + ends(misc) + jnp.where(sub < 4, yr[1, ring], yr[0, ring])
            elif j == 2:
                third = third + ends(turn(misc, 6))
            elif j == 1:
                third = third + ends(turn(misc, 4))
            for i in range(nt):
                s = slice(8 * i, 8 * i + 8)
                p0[x + H, s, :] = tiles[i] + p0[x + H, s, :] if j >= 3 else tiles[i]
            s = slice(cy, rows)
            p0[x + H, s, :] = third + p0[x + H, s, :] if j == 4 else third

    diag = ((4.0 + HELMHOLTZ) * rho + face + face_dn) / 6.0 - 1.0
    rho6, face6, face_dn6 = rho / 6.0, face / 6.0, face_dn / 6.0

    def scaled(f, x):
        c = f[x]
        side = f[x + 1] + f[x - 1] + north(c) + south(c)
        return diag * c - rho6 * side - face6 * up(c) - face_dn6 * down(c)

    def step1(x):
        p1[x] = scaled(p0, x)

    def step2(x):
        p2[x] = 2.0 * scaled(p1, x) - p0[x]

    def step3(x):
        p3[x] = 2.0 * scaled(p2, x) - p1[x]

    full = cx + 2 * H
    sweep(1, full - 1, step1, 30)
    sweep(2, full - 2, step2, 30)
    sweep(3, full - 3, step3, 30)

    def dots(x, acc):
        a0, a1, a2, a3 = p0[x, 0:cy, :], p1[x, 0:cy, :], p2[x, 0:cy, :], p3[x]
        a4 = 2.0 * scaled(p3, x)[:cy] - a2
        a3 = a3[:cy]
        pairs = ((a0, a0), (a0, a1), (a1, a1), (a1, a2), (a2, a2), (a2, a3), (a3, a3), (a3, a4))
        return tuple(s + f * g for s, (f, g) in zip(acc, pairs))

    def dots_some(i, acc):
        for j in range(12):
            acc = dots(H + 12 * i + j, acc)
        return acc

    acc = lax.fori_loop(0, cx // 12, dots_some, (jnp.zeros((cy, nz), jnp.float32),) * 8)
    for x in range(cx // 12 * 12, cx):
        acc = dots(H + x, acc)
    corner = lax.broadcasted_iota(jnp.int32, (8, nz), 0) == lax.broadcasted_iota(
        jnp.int32, (8, nz), 1
    )
    sums = jnp.concatenate([jnp.sum(a, axis=0, keepdims=True) for a in acc], axis=0)
    sums = jnp.sum(sums, axis=1, keepdims=True)
    part[...] = jnp.sum(jnp.where(corner, sums, 0.0), axis=0, keepdims=True)
    got_x[me] = part[...]

    def share(target):
        pltpu.make_async_remote_copy(
            src_ref=part, dst_ref=got_x.at[me], send_sem=sum_send, recv_sem=sum_recv,
            device_id=target, device_id_type=MESH,
        ).start()

    visit(share)
    bulk = got_x.at[pl.ds(0, everyone - 1)]

    for copy in sides + moves:
        copy.wait_recv()
    half = nz // 2
    nlev = KHI - KLO
    for o in range(ngx):
        r = slice(o * slots, (o + 1) * slots)
        size_d[r, :] = dr[o, 0]
        mult_d[r, :] = dr[o, 1]
        cell = dr[o, 2].astype(jnp.int32)
        col_s[r, :] = cell // (2 * nz)
        pos_s[r, :] = (cell // nz) % 2 * nlev + cell % nz - KLO
    wide = lax.broadcasted_iota(jnp.int32, (half, dpb), 0)
    narrow = lax.broadcasted_iota(jnp.int32, (cx, dpb), 0)
    for r in range(nrow):
        one = jnp.where(wide == pos_s[r : r + 1, :], 1.0, 0.0).astype(jnp.bfloat16)
        hot_s[r, 0:half, :] = one
        hot_s[r, half:nz, :] = one

    pull = DT * 0.5

    def prepare(x):
        for i, p in enumerate((p0, p1, p2, p3)):
            tall = p[x + H]
            own = tall[:cy]
            grad[0, i, x] = pull * (p[x + H + 1, 0:cy, :] - p[x + H - 1, 0:cy, :])
            grad[1, i, x] = pull * (north(tall) - south(tall))[:cy]
            grad[2, i, x] = pull * (not_top * up(own) - not_bot * down(own))
        for k, f in enumerate((te, qe)):
            tall = f[x + 1]
            h = tall[:cy]
            slope[k, 0, x] = DT * (h - f[x, 0:cy, :])
            slope[k, 1, x] = DT * (f[x + 2, 0:cy, :] - h)
            slope[k, 2, x] = DT * (h - south(tall)[:cy])
            slope[k, 3, x] = DT * (north(tall)[:cy] - h)
            slope[k, 4, x] = DT * not_bot * (h - down(h))
            slope[k, 5, x] = DT * not_top * (up(h) - h)

    sweep(0, cx, prepare, 4)
    pltpu.make_async_copy(bulk, bulk, sum_recv).wait()
    total = got_x[0]
    for o in range(1, everyone):
        total = total + got_x[o]
    total = jnp.where(corner, total, 0.0)
    total = jnp.broadcast_to(jnp.sum(total, axis=1, keepdims=True), (8, nz))
    dot = [total[i : i + 1, :] for i in range(8)]
    m = [dot[0], dot[1]]
    for k in range(2, 8):
        m.append(2.0 * dot[k] - m[k % 2])
    c0, c1, c2, c3 = cg_coefficients(m)

    sub_y = lax.broadcasted_iota(jnp.int32, (cy, nz), 0)
    lanes = lax.broadcasted_iota(jnp.int32, (cy, nz), 1)
    even = sub_y % 2 == 0

    def advance(x):
        def wind(now, k):
            return now - (
                (c0 * grad[k, 0, x] + c1 * grad[k, 1, x]) + (c2 * grad[k, 2, x] + c3 * grad[k, 3, x])
            )

        u, v, w = wind(us[x + 2], 0), wind(vs[x], 1), wind(le[x], 2)
        uo_ref[x] = u
        vo_ref[x] = v
        wo_ref[x] = w
        u_in, v_in, w_in = u > 0.0, v > 0.0, w > 0.0

        def move(f, k):
            return f[x + 1, 0:cy, :] - (
                u * jnp.where(u_in, slope[k, 0, x], slope[k, 1, x])
                + v * jnp.where(v_in, slope[k, 2, x], slope[k, 3, x])
                + w * jnp.where(w_in, slope[k, 4, x], slope[k, 5, x])
            )

        tt, qq = move(te, 0), move(qe, 1)
        to_ref[x] = tt
        qo_ref[x] = qq
        sat = qq * jnp.exp(-CLAUSIUS_FACTOR * tt) - 1.0
        for i in range(nt):
            a, b = sat[8 * i : 8 * i + 8], tt[8 * i : 8 * i + 8]
            first_col = jnp.where(pair, a, turn(b, 1))
            second_col = jnp.where(pair, turn(a, 7), b)
            both = jnp.where(
                lane < nlev,
                pltpu.roll(first_col, nz - KLO, 1),
                pltpu.roll(second_col, nz - KLO + nlev, 1),
            )
            big = both.astype(jnp.bfloat16).astype(f32)
            packed[pl.ds(pl.multiple_of(x * cy + 8 * i, 8), 8), :] = jnp.where(
                lane < half, big, pltpu.roll(both - big, half, 1)
            )

    f32 = jnp.float32
    pair = sub % 2 == 0
    sweep(0, cx, advance, 24)
    for b in range(NBD):
        for k in range(2):
            blk[b, k * cx : (k + 1) * cx, :] = packed[pl.ds(2 * b + k, cx, stride=cy), :]

    first = 8 + len(started)

    def back(place, peer):
        return pltpu.make_async_remote_copy(
            src_ref=xb.at[peer], dst_ref=rb.at[gx],
            send_sem=send_sem.at[first + place], recv_sem=recv_sem.at[first + place],
            device_id=(grp, peer, gy), device_id_type=MESH,
        )

    def back_start(peer):
        back(lax.rem(peer - gx + ngx, ngx) - 1, peer).start()

    backs = [back(p, lax.rem(gx + p + 1, ngx)) for p in range(ngx - 1)]
    middle = ngx // 2
    for owners in (range(middle), range(middle, ngx)):
        span = slice(owners[0] * slots, (owners[-1] + 1) * slots)
        for r in range(span.start, span.stop):
            o, t = r // slots, r % slots
            table = None
            for b in range(t, NBD, slots):
                term = jnp.where(map_s[0, b] == o, 1.0, 0.0) * blk[b]
                table = term if table is None else table + term
            lhs = table.astype(jnp.bfloat16)
            res = jnp.dot(lhs, hot_s[r], preferred_element_type=f32)
            mask = narrow == col_s[r : r + 1, :]
            sat_s[r : r + 1, :] = jnp.sum(keep(mask, res[:cx]), axis=0, keepdims=True)
            tmp_s[r : r + 1, :] = jnp.sum(keep(mask, res[cx:]), axis=0, keepdims=True)
        rate = (2.0 * SUB_STEP * GROWTH) * jnp.exp(GROWTH_SLOPE * tmp_s[span, :])
        gain = rate * sat_s[span, :]
        loss = rate * CURVATURE
        new = size_d[span, :]
        for _ in range(NSUB):
            new = jnp.maximum(new + gain - loss * lax.rsqrt(new), FLOOR_SQUARE)
        grown_s[span, :] = new
        for peer in owners:
            k = (peer - owners[0]) * slots
            xb[peer] = new[k : k + slots]
        for peer in owners:
            pl.when(peer != gx)(functools.partial(back_start, peer))
    old, new = size_d[...], grown_s[...]
    rb[gx] = xb[gx]
    sat_s[...] = CONDENSE * mult_d[...] * (new * jnp.sqrt(new) - old * jnp.sqrt(old))

    across = (((1,), (1,)), ((), ()))
    for r in range(nrow):
        mass = sat_s[r : r + 1, :]
        big = mass.astype(jnp.bfloat16).astype(f32)
        mask = narrow == col_s[r : r + 1, :]
        both = jnp.concatenate([keep(mask, big), keep(mask, mass - big)], axis=0)
        res = lax.dot_general(
            both.astype(jnp.bfloat16), hot_s[r], across, preferred_element_type=f32
        )
        out2[r] = res[:cx] + res[cx:]

    for b in range(NBD):
        acc = None
        for o in range(ngx):
            term = jnp.where(map_s[0, b] == o, 1.0, 0.0) * out2[o * slots + b % slots]
            acc = term if acc is None else acc + term
        grid_c[pl.ds(2 * b, cx, stride=cy), :] = acc
        grid_c[pl.ds(2 * b + 1, cx, stride=cy), :] = acc
    cloudy = (lanes >= KLO) & (lanes < KHI)

    def column(x):
        f = grid_c[pl.ds(pl.multiple_of(x * cy, 8), cy), :]
        f = jnp.where(even, pltpu.roll(f, KLO, 1), pltpu.roll(f, KLO - nlev, 1))
        f = keep(cloudy, f)
        to_ref[x] += PHASE_WARMING * f
        qo_ref[x] -= f

    sweep(0, cx, column, 8)
    for copy in backs:
        copy.wait_recv()
    for o in range(ngx):
        r = slice(o * slots, (o + 1) * slots)
        so_ref[r, :] = jnp.where(living(o), rb[o], size_v[r, :])
    for copy in backs:
        copy.wait_send()
    pltpu.make_async_copy(bulk, bulk, sum_send).wait()
    drain()


def finish(*refs):
    sem = refs[-1]
    n = len(refs) // 2
    copies = [pltpu.make_async_copy(refs[i], refs[n + i], sem.at[i]) for i in range(n)]
    for copy in copies:
        copy.start()
    for copy in copies:
        copy.wait()


def on_device(ngrp, ngx, ngy, t, q, u, v, w, owner, count, size, mult, cell):
    cx, cy, nz = t.shape
    nrow, dpb = size.shape[2:]
    slots = nrow // ngx
    rows = cy + 8
    nt = cy // 8
    f32 = jnp.float32

    def buf(*shape):
        return pltpu.VMEM(shape, f32)

    ext = buf(cx + 2 * H, rows, nz)
    side = buf(cx + 2, rows, nz)
    grid = buf(cx, cy, nz)
    flat = buf(cx * cy, nz)
    vec = buf(nrow, dpb)
    ivec = pltpu.VMEM((nrow, dpb), jnp.int32)
    tables = buf(nrow, cx, nz)
    nsem = 12 + 2 * (ngx - 1)
    hbm = pl.BlockSpec(memory_space=pltpu.HBM)
    vm = pl.BlockSpec(memory_space=pltpu.VMEM)
    mid = pl.pallas_call(
        functools.partial(kernel, ngrp, ngx, ngy, slots),
        out_shape=(grid,) * 5 + (vec,),
        in_specs=[hbm] * 10,
        out_specs=(vm,) * 6,
        scratch_shapes=[
            buf(cx + 4, cy, nz), grid, grid, side, side, grid, ext, ext, ext, ext,
            buf(3, 4, cx, cy, nz), buf(2, 6, cx, cy, nz),
            vec, vec, ivec,
            pltpu.SMEM((1, NBD), jnp.int32), pltpu.SMEM((1, nrow), jnp.int32),
            buf(2, 5 * nt + 1, 8, nz), buf(2, 5 * nt + 1, 8, nz),
            buf(2, cx + 2, 8, nz), buf(2, cx + 2, 8, nz),
            buf(4, 2, 8, nz), buf(4, 2, 8, nz),
            buf(ngx, 3, slots, dpb), buf(ngx, 3, slots, dpb),
            buf(1, nz), buf(ngrp * ngx * ngy, 1, nz),
            buf(NBD, 2 * cx, nz), flat, ivec, ivec, vec, vec, vec, vec, vec,
            pltpu.VMEM((nrow, nz, dpb), jnp.bfloat16),
            buf(ngx, slots, dpb), buf(ngx, slots, dpb), tables, flat,
            pltpu.SemaphoreType.DMA((10,)),
            pltpu.SemaphoreType.DMA((nsem,)),
            pltpu.SemaphoreType.DMA((nsem,)),
            pltpu.SemaphoreType.DMA,
            pltpu.SemaphoreType.DMA,
        ],
        compiler_params=pltpu.CompilerParams(
            collective_id=0, has_side_effects=True, vmem_limit_bytes=24 * 2**20
        ),
        name="cloud_step",
    )(
        *(
            pltpu.with_memory_space_constraint(a, pltpu.HBM)
            for a in (
                t, q, u, v, w, owner.reshape(1, -1), count.reshape(1, -1),
                size[0, 0], mult[0, 0], cell[0, 0],
            )
        )
    )
    outs = pl.pallas_call(
        finish,
        out_shape=tuple(jax.ShapeDtypeStruct(a.shape, f32) for a in mid),
        in_specs=[vm] * 6,
        out_specs=(hbm,) * 6,
        scratch_shapes=[pltpu.SemaphoreType.DMA((6,))],
        compiler_params=pltpu.CompilerParams(vmem_limit_bytes=4 * 2**20),
        name="finish",
    )(*mid)
    return outs[:5] + (outs[5][None, None],)


def solution(mesh):
    grid = P(("grp", "gx"), "gy", None)
    drop = P(("grp", "gx"), "gy", None, None)
    return jax.shard_map(
        functools.partial(on_device, mesh.shape["grp"], mesh.shape["gx"], mesh.shape["gy"]),
        mesh=mesh,
        in_specs=(grid,) * 7 + (drop,) * 3,
        out_specs=(grid,) * 5 + (drop,),
        check_vma=False,
    )
```
